32 devices in a mesh: row: 8 (over z, x), col: 4 (over y, core).
Axes of the slice: x: 2, y: 2, z: 4, core: 2. Of those that a mesh axis runs over, the one named last changes fastest.
Arguments:
- gram_tiles: float32 [2, 8, 4, 4, 512, 512], P(None, 'row', None, 'col'), as said below
Outputs:
- factor_tiles: float32 [2, 8, 4, 4, 512, 512], P(None, 'row', None, 'col')
Inputs may be any that keep to these rules, and one draw needn't show every extreme that they name: gram_tiles holds a symmetric positive definite matrix with positive entries.
All inputs are finite; a program needn't handle non-finite values.
Results may differ from the reference program's by a relative error of at most 0.0001.
Values sent between devices are 32-bit elements; how exact they have to be, the bound alone decides.
No kernel may reach another device: no remote copies, remote signals or barrier semaphores. Data moves between devices by JAX's collectives and lax.ppermute only.
A program may use at most 128 MiB of HBM per device.

```python
import math
import jax
import jax.numpy as jnp
from jax import lax

B = 512
TPR = 2
STEPS = 2
NT = 16
TPC = 4
N_ROW = 8
N_COL = 4


def draw_gram_tiles(key, part):
    order = NT * B
    first_key = jax.random.fold_in(key, 0)
    second_key = jax.random.fold_in(key, 1)
    fourth_key = jax.random.fold_in(key, 3)
    fifth_key = jax.random.fold_in(key, 4)
    noise = jax.random.uniform(first_key, (order, order), jnp.float32)
    first_factor = jax.random.uniform(fourth_key, (order,), jnp.float32, -1.0, 1.0)
    second_factor = jax.random.uniform(fifth_key, (order,), jnp.float32, -1.0, 1.0)
    shared = first_factor[:, None] * first_factor[None, :] + second_factor[:, None] * second_factor[None, :]
    coupling = 1.0 + 0.25 * (noise + noise.T - 1.0) + 0.35 * shared
    ridge = 0.5 * math.sqrt(order) * (1.0 + jax.random.uniform(second_key, (order,), jnp.float32))
    position = jnp.arange(order)
    matrix = jnp.where(position[:, None] == position[None, :], ridge[:, None], coupling)
    return matrix.reshape(TPR, NT // TPR, B, TPC, NT // TPC, B).transpose(0, 1, 3, 4, 2, 5)


def setup_inputs(seed: int = 0) -> dict:
    keys = jax.random.split(jax.random.key(seed), 2)
    return {
        "gram_tiles": draw_gram_tiles(jax.random.fold_in(keys[1], 71), 0),
    }


def to_matrix(tiles):
    return tiles.transpose(0, 1, 4, 2, 3, 5).reshape(NT * B, NT * B)

def from_matrix(matrix):
    return matrix.reshape(TPR, N_ROW, B, TPC, N_COL, B).transpose(0, 1, 3, 4, 2, 5)

def reference(gram_tiles):
    matrix = to_matrix(gram_tiles)
    for section in range(STEPS):
        begin_at = section * B
        end_at = begin_at + B
        factor = jnp.linalg.cholesky(matrix[begin_at:end_at, begin_at:end_at])
        panel = jax.scipy.linalg.solve_triangular(factor, matrix[end_at:, begin_at:end_at].T, lower=True).T
        product = jnp.dot(panel, panel.T, precision=lax.Precision.HIGHEST)
        matrix = matrix.at[end_at:, end_at:].set(matrix[end_at:, end_at:] - product)
        matrix = matrix.at[begin_at:end_at, begin_at:end_at].set(factor)
        matrix = matrix.at[end_at:, begin_at:end_at].set(panel)
        matrix = matrix.at[begin_at:end_at, end_at:].set(jnp.zeros((B, matrix.shape[0] - end_at), jnp.float32))
    return from_matrix(matrix)
```

```python
import functools

import jax
import jax.numpy as jnp
from jax import lax
from jax.experimental import pallas as pl
from jax.experimental.pallas import tpu as pltpu
from jax.sharding import PartitionSpec as P

GROUP = 8
BLOCK = 128
AXES = ("row", "col")
BULK = lax.Precision.HIGH


def contract(a, b, ca, cb, precision=lax.Precision.HIGHEST):
    return lax.dot_general(
        a, b, (((ca,), (cb,)), ((), ())), precision=precision, preferred_element_type=jnp.float32
    )


def reciprocal_root(value):
    guess = lax.rsqrt(value)
    return guess * (1.5 - 0.5 * value * guess * guess)


def factor_block(s_ref, e_ref, u_ref):
    n = s_ref.shape[0]
    sub = lax.broadcasted_iota(jnp.int32, (GROUP, n), 0)
    lane = lax.broadcasted_iota(jnp.int32, (GROUP, n), 1)
    down = lax.broadcasted_iota(jnp.int32, (n, n), 0)
    across = lax.broadcasted_iota(jnp.int32, (n, n), 1)
    e_ref[...] = (down == across).astype(jnp.float32)
    for start in range(0, n, GROUP):
        stop = start + GROUP
        tall = s_ref[start:stop, :]
        unit = e_ref[start:stop, :]
        entry = {}
        for j in range(GROUP):
            for i in range(j, GROUP):
                entry[i, j] = jnp.broadcast_to(tall[j : j + 1, start + i : start + i + 1], (1, n))
        rows = [tall[t : t + 1, :] for t in range(GROUP)]
        units = [unit[t : t + 1, :] for t in range(GROUP)]
        for t in range(GROUP):
            scale = reciprocal_root(entry[t, t])
            for i in range(t + 1, GROUP):
                entry[i, t] = entry[i, t] * scale
            rows[t] = rows[t] * scale
            units[t] = units[t] * scale
            for i in range(t + 1, GROUP):
                for j in range(t + 1, i + 1):
                    entry[i, j] = entry[i, j] - entry[i, t] * entry[j, t]
                rows[i] = rows[i] - entry[i, t] * rows[t]
                units[i] = units[i] - entry[i, t] * units[t]
        u = jnp.where(lane >= sub + start, jnp.concatenate(rows, 0), 0.0)
        v = jnp.concatenate(units, 0)
        u_ref[start:stop, :] = u
        e_ref[start:stop, :] = v
        if stop < n:
            s_ref[stop:, :] = s_ref[stop:, :] - contract(u, u, 0, 0)[stop:, :]
            e_ref[stop:, :] = e_ref[stop:, :] - contract(u, v, 0, 0)[stop:, :]


def eliminate(first, last, a_ref, l_ref, w_ref, s_ref, e_ref, u_ref):
    n = a_ref.shape[0]
    rows = lax.broadcasted_iota(jnp.int32, (n, BLOCK), 0)

    def body(k, carry):
        offset = pl.multiple_of(k * BLOCK, BLOCK)
        at = pl.ds(offset, BLOCK)
        s_ref[...] = a_ref[at, at]
        factor_block(s_ref, e_ref, u_ref)
        inverse = e_ref[...]
        below = jnp.where(rows >= offset + BLOCK, contract(a_ref[:, at], inverse, 1, 1), 0.0)
        l_ref[:, at] = below
        l_ref[at, at] = u_ref[...].T
        solved = contract(inverse, w_ref[at, :], 1, 0)
        w_ref[at, :] = solved
        a_ref[...] -= contract(below, below, 1, 1)
        w_ref[...] -= contract(below, solved, 1, 0)
        return carry

    lax.fori_loop(first, last, body, 0)


def start_w(w_ref):
    n = w_ref.shape[0]
    down = lax.broadcasted_iota(jnp.int32, (n, n), 0)
    across = lax.broadcasted_iota(jnp.int32, (n, n), 1)
    w_ref[...] = (down == across).astype(jnp.float32)


def open_kernel(last, x_ref, a_ref, l_ref, w_ref, *scratch):
    a_ref[...] = x_ref[...]
    start_w(w_ref)
    eliminate(0, last, a_ref, l_ref, w_ref, *scratch)


def corner_kernel(last, side_ref, x_ref, inverse_ref, p_ref, a_ref, l_ref, w_ref, *scratch):
    p = contract(side_ref[...], inverse_ref[...], 1, 1)
    p_ref[...] = p
    a_ref[...] = x_ref[...] - contract(p, p, 1, 1)
    start_w(w_ref)
    eliminate(0, last, a_ref, l_ref, w_ref, *scratch)


def close_kernel(first, last, a_in, l_in, w_in, l_ref, w_ref, a_ref, *scratch):
    a_ref[...] = a_in[...]
    l_ref[...] = l_in[...]
    w_ref[...] = w_in[...]
    eliminate(first, last, a_ref, l_ref, w_ref, *scratch)


def call(kernel, n, inputs, outputs, extra=()):
    tile = jax.ShapeDtypeStruct((n, n), jnp.float32)
    small = pltpu.VMEM((BLOCK, BLOCK), jnp.float32)
    space = pl.BlockSpec(memory_space=pltpu.VMEM)
    return pl.pallas_call(
        kernel,
        out_shape=[tile] * outputs,
        in_specs=[space] * len(inputs),
        out_specs=[space] * outputs,
        scratch_shapes=[*extra, small, small, small],
        cost_estimate=pl.CostEstimate(flops=20_000_000_000, bytes_accessed=60_000_000, transcendentals=0),
    )(*inputs)


def factor_first(x):
    n = x.shape[0]
    half = n // BLOCK // 2
    a, l, w = call(functools.partial(open_kernel, half), n, (x,), 3)
    return close(a, l, w)


def close(a, l, w):
    n = a.shape[0]
    half = n // BLOCK // 2
    extra = (pltpu.VMEM((n, n), jnp.float32),)
    return call(functools.partial(close_kernel, half, n // BLOCK), n, (a, l, w), 2, extra)


def factor_second(side, x, inverse):
    n = x.shape[0]
    half = n // BLOCK // 2
    p, a, l, w = call(functools.partial(corner_kernel, half), n, (side, x, inverse), 4)
    return p, *close(a, l, w)


class Grid:
    def __init__(self):
        self.rows = lax.axis_size("row")
        self.cols = lax.axis_size("col")
        self.his = self.rows // 2
        self.ys = self.cols // 2
        row = lax.axis_index("row")
        col = lax.axis_index("col")
        self.row, self.col = row, col
        self.hi, self.lo, self.y, self.core = row // 2, row % 2, col // 2, col % 2

    def send(self, x, target):
        pairs = []
        for hi in range(self.his):
            for lo in range(2):
                for y in range(self.ys):
                    for core in range(2):
                        to = target(hi, lo, y, core)
                        if to is not None:
                            pairs.append((self.number(hi, lo, y, core), self.number(*to)))
        return lax.ppermute(x, AXES, pairs)

    def number(self, hi, lo, y, core):
        return (hi * 2 + lo) * self.cols + y * 2 + core

    def swap_lo(self, x):
        return self.send(x, lambda hi, lo, y, core: (hi, 1 - lo, y, core))

    def swap_core(self, x):
        return self.send(x, lambda hi, lo, y, core: (hi, lo, y, 1 - core))

    def swap_y(self, x, s):
        return self.send(x, lambda hi, lo, y, core: (hi, lo, y ^ s, core))

    def swap_hi(self, x, s):
        return self.send(x, lambda hi, lo, y, core: (hi ^ s, lo, y, core))


def share_corner(grid, tile):
    n = tile.shape[0]
    count = n // BLOCK
    total = grid.rows * grid.cols
    at = [(i, j) for i in range(count) for j in range(i + 1)]
    blocks = [tile[i * BLOCK : (i + 1) * BLOCK, j * BLOCK : (j + 1) * BLOCK] for i, j in at]
    packed = jnp.stack(blocks).reshape(total, -1, BLOCK)
    mine = lax.all_to_all(packed, AXES, 0, 0, tiled=True)[0]
    spread = jnp.broadcast_to(mine[None], packed.shape)
    packed = lax.all_to_all(spread, AXES, 0, 0, tiled=True).reshape(len(at), BLOCK, BLOCK)
    zero = jnp.zeros((BLOCK, BLOCK), jnp.float32)
    lookup = {key: packed[k] for k, key in enumerate(at)}
    return jnp.concatenate(
        [jnp.concatenate([lookup.get((i, j), zero) for j in range(count)], 1) for i in range(count)], 0
    )


def share_side(grid, tile):
    n = tile.shape[0]
    pieces = tile.reshape(2, grid.ys, n // (2 * grid.ys), n)
    got = grid.send(pieces[0], lambda hi, lo, y, core: (0, 0, 0, core) if (hi, lo, y) == (0, 1, 0) else None)
    half = jnp.where(grid.lo == 1, pieces[1], got)
    piece = half[0]
    for h in range(1, grid.ys):
        got = grid.send(half[h], lambda hi, lo, y, core: (0, lo, h, core) if (hi, y) == (0, 0) else None)
        piece = jnp.where(grid.y == h, got, piece)
    first = piece
    for h in range(1, grid.his):
        got = grid.send(first, lambda hi, lo, y, core: (h, lo, y, core) if hi == 0 else None)
        piece = jnp.where(grid.hi == h, got, piece)
    others = [piece] + [grid.swap_y(piece, s) for s in range(1, grid.ys)]
    parts = []
    for h in range(grid.ys):
        part = others[0]
        for s in range(1, grid.ys):
            part = jnp.where(grid.y ^ s == h, others[s], part)
        parts.append(part)
    half = jnp.stack(parts)
    other = grid.swap_lo(half)
    low = grid.lo == 0
    whole = jnp.stack([jnp.where(low, half, other), jnp.where(low, other, half)]).reshape(n, n)
    other = grid.swap_core(whole)
    even = grid.core == 0
    return jnp.where(even, whole, other), jnp.where(even, other, whole)


def share_panels(grid, column):
    slots = column.shape[0]
    even = grid.core == 0
    own, near, far = [], [], []
    for a in range(slots):
        tile = column[a]
        for h in range(1, grid.ys):
            got = grid.send(column[a], lambda hi, lo, y, core: (hi, lo, h, core) if y == 0 else None)
            tile = jnp.where(grid.y == h, got, tile)
        own.append(tile)
        same = tile
        for s in range(1, grid.ys):
            got = grid.swap_hi(tile, s)
            same = jnp.where((grid.hi % grid.ys) ^ grid.y == s, got, same)
        near.append(same)
        if grid.ys == 2:
            middle = grid.send(same, lambda hi, lo, y, core: (3 - hi, lo, y, core) if hi in (1, 2) else None)
            edge = grid.swap_hi(middle, 1)
            far.append(jnp.where((grid.hi == 1) | (grid.hi == 2), middle, edge))
        else:
            far.append(grid.swap_hi(same, grid.ys))
    keep, give = [], []
    mine = grid.lo == grid.core
    for a in range(slots):
        for tile in (near[a], far[a]):
            other = grid.swap_lo(tile)
            keep.append(jnp.where(mine, tile, other))
            give.append(jnp.where(mine, other, tile))
    keep = jnp.stack(keep)
    got = grid.swap_core(jnp.stack(give))
    first = (grid.hi // grid.ys) == 0

    def ordered(x):
        x = x.reshape(slots, 2, *x.shape[1:])
        return jnp.where(first, x, x[:, ::-1]).reshape(2 * slots, *x.shape[2:])

    columns = [ordered(jnp.where(even, keep, got)), ordered(jnp.where(even, got, keep))]
    own = jnp.stack(own)
    got = grid.swap_core(own)
    rows = [jnp.where(even, own, got), jnp.where(even, got, own)]
    return rows, columns


def shards(gram_tiles):
    blocks = gram_tiles[:, 0, :, 0]
    grid = Grid()
    n = blocks.shape[-1]
    column = blocks[:, 0]
    corner = share_corner(grid, blocks[0, 0])
    side, last = share_side(grid, blocks[0, 0])
    rows, columns = share_panels(grid, column)
    l0, w0 = factor_first(corner)
    l10, l1, w1 = factor_second(side, last, w0)

    count = blocks.shape[0]
    raw0 = jnp.concatenate([rows[0], columns[0]]).reshape(-1, n)
    raw1 = jnp.concatenate([rows[1], columns[1]]).reshape(-1, n)
    p0 = contract(raw0, w0, 1, 1, BULK)
    p1 = contract(raw1 - contract(p0, l10, 1, 1, BULK), w1, 1, 1, BULK)
    panel = jnp.concatenate([p0, p1], 1)
    update = contract(panel[: count * n], panel[count * n :], 1, 1, BULK)
    update = update.reshape(count, n, -1, n).transpose(0, 2, 1, 3)
    blocks = blocks - update

    p0 = p0[: count * n].reshape(count, 1, n, n)
    p1 = p1[: count * n].reshape(count, 1, n, n)
    row_ids = (jnp.arange(count, dtype=jnp.int32) * grid.rows + grid.row)[:, None, None, None]
    col_ids = (jnp.arange(blocks.shape[1], dtype=jnp.int32) * grid.cols + grid.col)[None, :, None, None]
    blocks = jnp.where(col_ids == 0, p0, blocks)
    blocks = jnp.where(col_ids == 1, p1, blocks)
    blocks = jnp.where((row_ids == 0) | ((row_ids == 1) & (col_ids > 1)), 0.0, blocks)
    blocks = jnp.where((row_ids == 0) & (col_ids == 0), l0, blocks)
    blocks = jnp.where((row_ids == 1) & (col_ids == 0), l10, blocks)
    blocks = jnp.where((row_ids == 1) & (col_ids == 1), l1, blocks)
    return blocks[:, None, :, None]


def solution(mesh):
    placed = P(None, "row", None, "col", None, None)
    return jax.shard_map(shards, mesh=mesh, in_specs=(placed,), out_specs=placed, check_vma=False)
```

```python
import functools

import jax
import jax.numpy as jnp
from jax import lax
from jax.experimental import pallas as pl
from jax.experimental.pallas import tpu as pltpu
from jax.sharding import PartitionSpec as P

GROUP = 16
BLOCK = 128
AXES = ("row", "col")


def contract(a, b, ca, cb, precision=lax.Precision.HIGHEST):
    return lax.dot_general(
        a, b, (((ca,), (cb,)), ((), ())), precision=precision, preferred_element_type=jnp.float32
    )


def reciprocal_root(value):
    guess = lax.rsqrt(value)
    return guess * (1.5 - 0.5 * value * guess * guess)


def factor_block(s_ref, e_ref, u_ref):
    n = s_ref.shape[0]
    sub = lax.broadcasted_iota(jnp.int32, (GROUP, n), 0)
    lane = lax.broadcasted_iota(jnp.int32, (GROUP, n), 1)
    down = lax.broadcasted_iota(jnp.int32, (n, n), 0)
    across = lax.broadcasted_iota(jnp.int32, (n, n), 1)
    e_ref[...] = (down == across).astype(jnp.float32)
    for start in range(0, n, GROUP):
        stop = start + GROUP
        tall = s_ref[start:stop, :]
        unit = e_ref[start:stop, :]
        entry = {}
        for j in range(GROUP):
            for i in range(j, GROUP):
                entry[i, j] = jnp.broadcast_to(tall[j : j + 1, start + i : start + i + 1], (1, n))
        rows = [tall[t : t + 1, :] for t in range(GROUP)]
        units = [unit[t : t + 1, :] for t in range(GROUP)]
        for t in range(GROUP):
            scale = reciprocal_root(entry[t, t])
            for i in range(t + 1, GROUP):
                entry[i, t] = entry[i, t] * scale
            rows[t] = rows[t] * scale
            units[t] = units[t] * scale
            for i in range(t + 1, GROUP):
                for j in range(t + 1, i + 1):
                    entry[i, j] = entry[i, j] - entry[i, t] * entry[j, t]
                rows[i] = rows[i] - entry[i, t] * rows[t]
                units[i] = units[i] - entry[i, t] * units[t]
        u = jnp.where(lane >= sub + start, jnp.concatenate(rows, 0), 0.0)
        v = jnp.concatenate(units, 0)
        u_ref[start:stop, :] = u
        e_ref[start:stop, :] = v
        if stop < n:
            s_ref[stop:, :] = s_ref[stop:, :] - contract(u, u, 0, 0)[stop:, :]
            e_ref[stop:, :] = e_ref[stop:, :] - contract(u, v, 0, 0)[stop:, :]


def eliminate(first, last, a_ref, l_ref, w_ref, s_ref, e_ref, u_ref):
    n = a_ref.shape[0]
    rows = lax.broadcasted_iota(jnp.int32, (n, BLOCK), 0)

    def body(k, carry):
        offset = pl.multiple_of(k * BLOCK, BLOCK)
        at = pl.ds(offset, BLOCK)
        s_ref[...] = a_ref[at, at]
        factor_block(s_ref, e_ref, u_ref)
        inverse = e_ref[...]
        below = jnp.where(rows >= offset + BLOCK, contract(a_ref[:, at], inverse, 1, 1), 0.0)
        l_ref[:, at] = below
        l_ref[at, at] = u_ref[...].T
        solved = contract(inverse, w_ref[at, :], 1, 0)
        w_ref[at, :] = solved
        a_ref[...] -= contract(below, below, 1, 1)
        w_ref[...] -= contract(below, solved, 1, 0)
        return carry

    lax.fori_loop(first, last, body, 0)


def start_w(w_ref):
    n = w_ref.shape[0]
    down = lax.broadcasted_iota(jnp.int32, (n, n), 0)
    across = lax.broadcasted_iota(jnp.int32, (n, n), 1)
    w_ref[...] = (down == across).astype(jnp.float32)


def open_kernel(last, x_ref, a_ref, l_ref, w_ref, *scratch):
    a_ref[...] = x_ref[...]
    start_w(w_ref)
    eliminate(0, last, a_ref, l_ref, w_ref, *scratch)


def corner_kernel(last, side_ref, x_ref, inverse_ref, p_ref, a_ref, l_ref, w_ref, *scratch):
    p = contract(side_ref[...], inverse_ref[...], 1, 1)
    p_ref[...] = p
    a_ref[...] = x_ref[...] - contract(p, p, 1, 1)
    start_w(w_ref)
    eliminate(0, last, a_ref, l_ref, w_ref, *scratch)


def close_kernel(first, last, a_in, l_in, w_in, l_ref, w_ref, a_ref, *scratch):
    a_ref[...] = a_in[...]
    l_ref[...] = l_in[...]
    w_ref[...] = w_in[...]
    eliminate(first, last, a_ref, l_ref, w_ref, *scratch)


def call(kernel, n, inputs, outputs, extra=()):
    tile = jax.ShapeDtypeStruct((n, n), jnp.float32)
    small = pltpu.VMEM((BLOCK, BLOCK), jnp.float32)
    space = pl.BlockSpec(memory_space=pltpu.VMEM)
    return pl.pallas_call(
        kernel,
        out_shape=[tile] * outputs,
        in_specs=[space] * len(inputs),
        out_specs=[space] * outputs,
        scratch_shapes=[*extra, small, small, small],
        cost_estimate=pl.CostEstimate(flops=20_000_000_000, bytes_accessed=60_000_000, transcendentals=0),
    )(*inputs)


def factor_first(x):
    n = x.shape[0]
    half = n // BLOCK // 2
    a, l, w = call(functools.partial(open_kernel, half), n, (x,), 3)
    return close(a, l, w)


def close(a, l, w):
    n = a.shape[0]
    half = n // BLOCK // 2
    extra = (pltpu.VMEM((n, n), jnp.float32),)
    return call(functools.partial(close_kernel, half, n // BLOCK), n, (a, l, w), 2, extra)


def factor_second(side, x, inverse):
    n = x.shape[0]
    half = n // BLOCK // 2
    p, a, l, w = call(functools.partial(corner_kernel, half), n, (side, x, inverse), 4)
    return p, *close(a, l, w)


class Grid:
    def __init__(self):
        self.rows = lax.axis_size("row")
        self.cols = lax.axis_size("col")
        self.his = self.rows // 2
        self.ys = self.cols // 2
        row = lax.axis_index("row")
        col = lax.axis_index("col")
        self.row, self.col = row, col
        self.hi, self.lo, self.y, self.core = row // 2, row % 2, col // 2, col % 2

    def send(self, x, target):
        pairs = []
        for hi in range(self.his):
            for lo in range(2):
                for y in range(self.ys):
                    for core in range(2):
                        to = target(hi, lo, y, core)
                        if to is not None:
                            pairs.append((self.number(hi, lo, y, core), self.number(*to)))
        return lax.ppermute(x, AXES, pairs)

    def number(self, hi, lo, y, core):
        return (hi * 2 + lo) * self.cols + y * 2 + core

    def swap_lo(self, x):
        return self.send(x, lambda hi, lo, y, core: (hi, 1 - lo, y, core))

    def swap_core(self, x):
        return self.send(x, lambda hi, lo, y, core: (hi, lo, y, 1 - core))

    def swap_y(self, x, s):
        return self.send(x, lambda hi, lo, y, core: (hi, lo, y ^ s, core))

    def swap_hi(self, x, s):
        return self.send(x, lambda hi, lo, y, core: (hi ^ s, lo, y, core))


def after(x, *values):
    return lax.optimization_barrier((x, *values))[0]


def corner_start(grid, tile):
    n = tile.shape[0]
    at = [(i, j) for i in range(n // BLOCK) for j in range(i + 1)]
    blocks = [tile[i * BLOCK : (i + 1) * BLOCK, j * BLOCK : (j + 1) * BLOCK] for i, j in at]
    packed = jnp.stack(blocks).reshape(grid.rows * grid.cols, -1, BLOCK)
    return lax.all_to_all(packed, AXES, 0, 0, tiled=True)[0]


def corner_finish(grid, mine, n):
    count = n // BLOCK
    at = [(i, j) for i in range(count) for j in range(i + 1)]
    spread = jnp.broadcast_to(mine[None], (grid.rows * grid.cols, *mine.shape))
    packed = lax.all_to_all(spread, AXES, 0, 0, tiled=True).reshape(len(at), BLOCK, BLOCK)
    zero = jnp.zeros((BLOCK, BLOCK), jnp.float32)
    lookup = {key: packed[k] for k, key in enumerate(at)}
    return jnp.concatenate(
        [jnp.concatenate([lookup.get((i, j), zero) for j in range(count)], 1) for i in range(count)], 0
    )


class Side:
    def __init__(self, grid, tile):
        self.grid = grid
        self.n = tile.shape[0]
        self.pieces = tile.reshape(2, grid.ys, self.n // (2 * grid.ys), self.n)

    def scatter(self):
        grid = self.grid
        got = grid.send(
            self.pieces[0], lambda hi, lo, y, core: (0, 0, 0, core) if (hi, lo, y) == (0, 1, 0) else None
        )
        half = jnp.where(grid.lo == 1, self.pieces[1], got)
        piece = half[0]
        for h in range(1, grid.ys):
            got = grid.send(half[h], lambda hi, lo, y, core: (0, lo, h, core) if (hi, y) == (0, 0) else None)
            piece = jnp.where(grid.y == h, got, piece)
        self.first = piece

    def climb(self):
        grid = self.grid
        self.climbed = [
            grid.send(self.first, lambda hi, lo, y, core: (h, lo, y, core) if hi == 0 else None)
            for h in range(1, grid.his)
        ]

    def gather_y(self, *values):
        grid = self.grid
        piece = self.first
        for h in range(1, grid.his):
            piece = jnp.where(grid.hi == h, after(self.climbed[h - 1], *values), piece)
        self.others = [piece] + [grid.swap_y(piece, s) for s in range(1, grid.ys)]

    def gather_lo(self, *values):
        grid = self.grid
        others = self.others[:1] + [after(x, *values) for x in self.others[1:]]
        parts = []
        for h in range(grid.ys):
            part = others[0]
            for s in range(1, grid.ys):
                part = jnp.where(grid.y ^ s == h, others[s], part)
            parts.append(part)
        self.half = jnp.stack(parts)
        self.other = grid.swap_lo(self.half)

    def finish(self, *values):
        grid = self.grid
        other = after(self.other, *values)
        low = grid.lo == 0
        whole = jnp.stack([jnp.where(low, self.half, other), jnp.where(low, other, self.half)])
        whole = whole.reshape(self.n, self.n)
        other = grid.swap_core(whole)
        even = grid.core == 0
        return jnp.where(even, whole, other), jnp.where(even, other, whole)


def split(x):
    high = x.astype(jnp.bfloat16)
    return high, (x - high.astype(jnp.float32)).astype(jnp.bfloat16)


def product(a, b, cb):
    def one(x, y):
        return lax.dot_general(x, y, (((1,), (cb,)), ((), ())), preferred_element_type=jnp.float32)

    return one(a[0], b[0]) + (one(a[0], b[1]) + one(a[1], b[0]))


def finish_kernel(shape, scalars, *refs):
    count, width, n = shape
    cols = count * 2
    total = count + cols
    g_ref, l0_ref, l10_ref, l1_ref, w0_ref, w1_ref = refs[:6]
    own = refs[6 : 6 + count]
    own_got = refs[6 + count : 6 + 2 * count]
    rest = refs[6 + 2 * count :]
    groups = [rest[k * count : (k + 1) * count] for k in range(8)]
    rest = rest[8 * count :]
    out_ref = rest[0]
    raw, high, low, keep, w0h, w0l, w1h, w1l, lh, ll, gbuf, obuf, rsem, gsem, osem = rest[1:]
    near, near_got, near_x, near_x_got, far, far_got, far_x, far_x_got = groups
    second_core, same_lo, second_half, row0, row1, col0 = [scalars[k] for k in range(6)]

    def fetch(options, slot, panel):
        for condition, ref in options:

            @pl.when(condition)
            def _():
                pltpu.make_async_copy(ref, raw.at[slot, panel], rsem.at[slot, panel]).start()

    for panel in range(2):
        mine = second_core == panel
        for a in range(count):
            fetch([(mine, own[a]), (jnp.logical_not(mine), own_got[a])], a, panel)
    for a in range(count):
        for block in range(2):
            local = second_half == block
            straight = same_lo == 1
            for panel in range(2):
                mine = second_core == panel
                options = []
                for is_near, sets in ((True, (near, near_got, near_x, near_x_got)), (False, (far, far_got, far_x, far_x_got))):
                    place = local if is_near else jnp.logical_not(local)
                    for is_straight, pair in ((True, sets[:2]), (False, sets[2:])):
                        way = straight if is_straight else jnp.logical_not(straight)
                        both = jnp.logical_and(place, way)
                        options.append((jnp.logical_and(both, mine), pair[0][a]))
                        options.append((jnp.logical_and(both, jnp.logical_not(mine)), pair[1][a]))
                fetch(options, count + 2 * a + block, panel)

    def g_copy(k, slot):
        return pltpu.make_async_copy(g_ref.at[k // width, k % width], gbuf.at[slot], gsem.at[slot])

    def o_copy(k, slot):
        return pltpu.make_async_copy(obuf.at[slot], out_ref.at[k // width, k % width], osem.at[slot])

    g_copy(0, 0).start()
    w0h[...], w0l[...] = split(w0_ref[...])
    w1h[...], w1l[...] = split(w1_ref[...])
    lh[...], ll[...] = split(l10_ref[...])

    def solve(k, carry):
        pltpu.make_async_copy(own[0], raw.at[k, 0], rsem.at[k, 0]).wait()
        p0 = product(split(raw[k, 0]), (w0h[...], w0l[...]), 1)
        pair = split(p0)
        high[k, 0] = pair[0]
        low[k, 0] = pair[1]
        pltpu.make_async_copy(own[0], raw.at[k, 1], rsem.at[k, 1]).wait()
        left = raw[k, 1] - product(pair, (lh[...], ll[...]), 1)
        p1 = product(split(left), (w1h[...], w1l[...]), 1)
        high[k, 1], low[k, 1] = split(p1)

        @pl.when(k < count)
        def _():
            keep[k, 0] = p0
            keep[k, 1] = p1

        return carry

    lax.fori_loop(0, total, solve, 0)

    def update(k, carry):
        slot = lax.rem(k, 2)
        a = k // width
        t = lax.rem(k, width)
        g_copy(k, slot).wait()

        @pl.when(k + 1 < count * width)
        def _():
            g_copy(k + 1, 1 - slot).start()

        @pl.when(k >= 2)
        def _():
            o_copy(k - 2, slot).wait()

        first_tile = jnp.logical_and(t == 0, col0 < 2)
        is_row0 = jnp.logical_and(a == 0, row0 == 1)
        is_row1 = jnp.logical_and(a == 0, row1 == 1)
        special = jnp.logical_or(is_row0, is_row1)

        @pl.when(jnp.logical_not(jnp.logical_or(first_tile, special)))
        def _():
            value = gbuf[slot]
            for panel in range(2):
                x = (high[a, panel], low[a, panel])
                y = (high[count + t, panel], low[count + t, panel])
                value = value - product(x, y, 1)
            obuf[slot] = value

        @pl.when(jnp.logical_and(special, jnp.logical_not(first_tile)))
        def _():
            obuf[slot] = jnp.zeros((n, n), jnp.float32)

        @pl.when(jnp.logical_and(first_tile, jnp.logical_not(special)))
        def _():
            obuf[slot] = keep[a, col0]

        @pl.when(jnp.logical_and(first_tile, is_row0))
        def _():
            obuf[slot] = jnp.where(col0 == 0, l0_ref[...], 0.0)

        @pl.when(jnp.logical_and(first_tile, is_row1))
        def _():
            obuf[slot] = jnp.where(col0 == 0, l10_ref[...], l1_ref[...])

        o_copy(k, slot).start()
        return carry

    last = count * width
    lax.fori_loop(0, last, update, 0)
    o_copy(last - 2, lax.rem(last, 2)).wait()
    o_copy(last - 1, lax.rem(last + 1, 2)).wait()


def finish(grid, blocks, factors, own, own_got, groups):
    count, width, n, _ = blocks.shape
    total = 3 * count
    scalars = jnp.stack(
        [
            grid.core,
            (grid.lo == grid.core).astype(jnp.int32),
            grid.hi // grid.ys,
            (grid.row == 0).astype(jnp.int32),
            (grid.row == 1).astype(jnp.int32),
            grid.col,
        ]
    ).astype(jnp.int32)
    inputs = [blocks, *factors, *own, *own_got]
    for group in groups:
        inputs += group
    anywhere = pl.BlockSpec(memory_space=pl.ANY)
    vmem = pl.BlockSpec(memory_space=pltpu.VMEM)
    half = pltpu.VMEM((n, n), jnp.bfloat16)
    return pl.pallas_call(
        functools.partial(finish_kernel, (count, width, n)),
        out_shape=jax.ShapeDtypeStruct(blocks.shape, jnp.float32),
        in_specs=[pl.BlockSpec(memory_space=pltpu.SMEM), anywhere] + [vmem] * 5 + [anywhere] * (len(inputs) - 6),
        out_specs=anywhere,
        scratch_shapes=[
            pltpu.VMEM((total, 2, n, n), jnp.float32),
            pltpu.VMEM((total, 2, n, n), jnp.bfloat16),
            pltpu.VMEM((total, 2, n, n), jnp.bfloat16),
            pltpu.VMEM((count, 2, n, n), jnp.float32),
            half,
            half,
            half,
            half,
            half,
            half,
            pltpu.VMEM((2, n, n), jnp.float32),
            pltpu.VMEM((2, n, n), jnp.float32),
            pltpu.SemaphoreType.DMA((total, 2)),
            pltpu.SemaphoreType.DMA((2,)),
            pltpu.SemaphoreType.DMA((2,)),
        ],
        compiler_params=pltpu.CompilerParams(vmem_limit_bytes=60 * 1024 * 1024),
    )(scalars, *inputs)


def shards(gram_tiles):
    blocks = gram_tiles[:, 0, :, 0]
    grid = Grid()
    n = blocks.shape[-1]
    half = n // BLOCK // 2
    slots = range(blocks.shape[0])
    raw = [blocks[a, 0] for a in slots]

    def up(a):
        return [grid.send(raw[a], lambda hi, lo, y, core: (hi, lo, h, core) if y == 0 else None) for h in range(1, grid.ys)]

    def own_tile(a, got):
        tile = raw[a]
        for h in range(1, grid.ys):
            tile = jnp.where(grid.y == h, got[h - 1], tile)
        return tile

    def pair_start(tile):
        return [grid.swap_hi(tile, s) for s in range(1, grid.ys)]

    def pair_finish(tile, got):
        same = tile
        for s in range(1, grid.ys):
            same = jnp.where((grid.hi % grid.ys) ^ grid.y == s, got[s - 1], same)
        return same

    def cross(tile):
        if grid.ys == 2:
            return grid.send(tile, lambda hi, lo, y, core: (3 - hi, lo, y, core) if hi in (1, 2) else None)
        return grid.swap_hi(tile, grid.ys)

    def spread(tile):
        return grid.swap_hi(tile, 1) if grid.ys == 2 else tile

    def far_tile(middle, edge):
        return jnp.where((grid.hi == 1) | (grid.hi == 2), middle, edge) if grid.ys == 2 else middle

    part = corner_start(grid, raw[0])
    side = Side(grid, raw[0])
    lifted = [up(a) for a in slots]
    side.scatter()
    corner = corner_finish(grid, part, n)
    own = [own_tile(0, lifted[0]), None]
    paired = [pair_start(own[0]), None]
    side.climb()

    got, lift = lax.optimization_barrier((paired[0], lifted[1]))
    near = [pair_finish(own[0], got), None]
    own[1] = own_tile(1, lift)
    paired[1] = pair_start(own[1])
    middle = [cross(near[0]), None]
    near_x = [grid.swap_lo(near[0]), None]
    x = after(corner, near[0], own[1])
    a, l, w = call(functools.partial(open_kernel, half), n, (x,), 3)

    side.gather_y(a)
    got, mid, nx = lax.optimization_barrier((paired[1], middle[0], near_x[0], a))[:3]
    middle[0], near_x[0] = mid, nx
    near[1] = pair_finish(own[1], got)
    edge = [spread(middle[0]), None]
    middle[1] = cross(near[1])
    near_x[1] = grid.swap_lo(near[1])
    a = after(a, near[1], side.others[0])
    l0, w0 = close(a, l, w)

    side.gather_lo(w0)
    own_got = [grid.swap_core(after(own[k], w0)) for k in slots]
    side0, side1 = side.finish(w0)
    mid, nx, eg = lax.optimization_barrier((middle[1], near_x[1], edge[0], w0))[:3]
    middle[1], near_x[1], edge[0] = mid, nx, eg
    far = [far_tile(middle[0], edge[0]), None]
    edge[1] = spread(middle[1])
    far_x = [grid.swap_lo(far[0]), None]
    near_got = [grid.swap_core(x) for x in near]
    near_x_got = [grid.swap_core(x) for x in near_x]
    side0 = after(side0, far[0])
    l10, a, l, w = call(functools.partial(corner_kernel, half), n, (side0, side1, w0), 4)

    eg, fx = lax.optimization_barrier((edge[1], far_x[0], a))[:2]
    edge[1], far_x[0] = eg, fx
    far[1] = far_tile(middle[1], edge[1])
    far_x[1] = grid.swap_lo(far[1])
    far_got = [grid.swap_core(x) for x in far]
    a = after(a, far[1])
    l1, w1 = close(a, l, w)

    fx = after(far_x[1], w1)
    far_x[1] = fx
    far_x_got = [grid.swap_core(x) for x in far_x]
    groups = [near, near_got, near_x, near_x_got, far, far_got, far_x, far_x_got]
    blocks = finish(grid, blocks, (l0, l10, l1, w0, w1), own, own_got, groups)
    return blocks[:, None, :, None]


def solution(mesh):
    placed = P(None, "row", None, "col", None, None)
    return jax.shard_map(shards, mesh=mesh, in_specs=(placed,), out_specs=placed, check_vma=False)
```

```python
import functools

import jax
import jax.numpy as jnp
from jax import lax
from jax.experimental import pallas as pl
from jax.experimental.pallas import tpu as pltpu
from jax.sharding import PartitionSpec as P

GROUP = 16
BLOCK = 128
AXES = ("row", "col")


def contract(a, b, ca, cb, precision=lax.Precision.HIGHEST):
    return lax.dot_general(
        a, b, (((ca,), (cb,)), ((), ())), precision=precision, preferred_element_type=jnp.float32
    )


def reciprocal_root(value):
    guess = lax.rsqrt(value)
    return guess * (1.5 - 0.5 * value * guess * guess)


def factor_block(s_ref, e_ref, u_ref):
    n = s_ref.shape[0]
    sub = lax.broadcasted_iota(jnp.int32, (GROUP, n), 0)
    lane = lax.broadcasted_iota(jnp.int32, (GROUP, n), 1)
    down = lax.broadcasted_iota(jnp.int32, (n, n), 0)
    across = lax.broadcasted_iota(jnp.int32, (n, n), 1)
    e_ref[...] = (down == across).astype(jnp.float32)
    for start in range(0, n, GROUP):
        stop = start + GROUP
        tall = s_ref[start:stop, :]
        unit = e_ref[start:stop, :]
        entry = {}
        for j in range(GROUP):
            for i in range(j, GROUP):
                entry[i, j] = jnp.broadcast_to(tall[j : j + 1, start + i : start + i + 1], (1, n))
        rows = [tall[t : t + 1, :] for t in range(GROUP)]
        units = [unit[t : t + 1, :] for t in range(GROUP)]
        for t in range(GROUP):
            scale = reciprocal_root(entry[t, t])
            for i in range(t + 1, GROUP):
                entry[i, t] = entry[i, t] * scale
            rows[t] = rows[t] * scale
            units[t] = units[t] * scale
            for i in range(t + 1, GROUP):
                for j in range(t + 1, i + 1):
                    entry[i, j] = entry[i, j] - entry[i, t] * entry[j, t]
                rows[i] = rows[i] - entry[i, t] * rows[t]
                units[i] = units[i] - entry[i, t] * units[t]
        u = jnp.where(lane >= sub + start, jnp.concatenate(rows, 0), 0.0)
        v = jnp.concatenate(units, 0)
        u_ref[start:stop, :] = u
        e_ref[start:stop, :] = v
        if stop < n:
            s_ref[stop:, :] = s_ref[stop:, :] - contract(u, u, 0, 0)[stop:, :]
            e_ref[stop:, :] = e_ref[stop:, :] - contract(u, v, 0, 0)[stop:, :]


def eliminate(first, last, a_ref, l_ref, w_ref, s_ref, e_ref, u_ref):
    n = a_ref.shape[0]
    rows = lax.broadcasted_iota(jnp.int32, (n, BLOCK), 0)

    def body(k, carry):
        offset = pl.multiple_of(k * BLOCK, BLOCK)
        at = pl.ds(offset, BLOCK)
        s_ref[...] = a_ref[at, at]
        factor_block(s_ref, e_ref, u_ref)
        inverse = e_ref[...]
        below = jnp.where(rows >= offset + BLOCK, contract(a_ref[:, at], inverse, 1, 1), 0.0)
        l_ref[:, at] = below
        l_ref[at, at] = u_ref[...].T
        solved = contract(inverse, w_ref[at, :], 1, 0)
        w_ref[at, :] = solved
        a_ref[...] -= contract(below, below, 1, 1)
        w_ref[...] -= contract(below, solved, 1, 0)
        return carry

    lax.fori_loop(first, last, body, 0)


def start_w(w_ref):
    n = w_ref.shape[0]
    down = lax.broadcasted_iota(jnp.int32, (n, n), 0)
    across = lax.broadcasted_iota(jnp.int32, (n, n), 1)
    w_ref[...] = (down == across).astype(jnp.float32)


def open_kernel(last, x_ref, a_ref, l_ref, w_ref, *scratch):
    a_ref[...] = x_ref[...]
    start_w(w_ref)
    eliminate(0, last, a_ref, l_ref, w_ref, *scratch)


def corner_kernel(last, side_ref, x_ref, inverse_ref, p_ref, a_ref, l_ref, w_ref, *scratch):
    p = contract(side_ref[...], inverse_ref[...], 1, 1)
    p_ref[...] = p
    a_ref[...] = x_ref[...] - contract(p, p, 1, 1)
    start_w(w_ref)
    eliminate(0, last, a_ref, l_ref, w_ref, *scratch)


def close_kernel(first, last, a_in, l_in, w_in, l_ref, w_ref, a_ref, *scratch):
    a_ref[...] = a_in[...]
    l_ref[...] = l_in[...]
    w_ref[...] = w_in[...]
    eliminate(first, last, a_ref, l_ref, w_ref, *scratch)


def call(kernel, n, inputs, outputs, extra=()):
    tile = jax.ShapeDtypeStruct((n, n), jnp.float32)
    small = pltpu.VMEM((BLOCK, BLOCK), jnp.float32)
    space = pl.BlockSpec(memory_space=pltpu.VMEM)
    return pl.pallas_call(
        kernel,
        out_shape=[tile] * outputs,
        in_specs=[space] * len(inputs),
        out_specs=[space] * outputs,
        scratch_shapes=[*extra, small, small, small],
        cost_estimate=pl.CostEstimate(flops=20_000_000_000, bytes_accessed=60_000_000, transcendentals=0),
    )(*inputs)


def factor_first(x):
    n = x.shape[0]
    half = n // BLOCK // 2
    a, l, w = call(functools.partial(open_kernel, half), n, (x,), 3)
    return close(a, l, w)


def close(a, l, w):
    n = a.shape[0]
    half = n // BLOCK // 2
    extra = (pltpu.VMEM((n, n), jnp.float32),)
    return call(functools.partial(close_kernel, half, n // BLOCK), n, (a, l, w), 2, extra)


def factor_second(side, x, inverse):
    n = x.shape[0]
    half = n // BLOCK // 2
    p, a, l, w = call(functools.partial(corner_kernel, half), n, (side, x, inverse), 4)
    return p, *close(a, l, w)


class Grid:
    def __init__(self):
        self.rows = lax.axis_size("row")
        self.cols = lax.axis_size("col")
        self.his = self.rows // 2
        self.ys = self.cols // 2
        row = lax.axis_index("row")
        col = lax.axis_index("col")
        self.row, self.col = row, col
        self.hi, self.lo, self.y, self.core = row // 2, row % 2, col // 2, col % 2

    def send(self, x, target):
        pairs = []
        for hi in range(self.his):
            for lo in range(2):
                for y in range(self.ys):
                    for core in range(2):
                        to = target(hi, lo, y, core)
                        if to is not None:
                            pairs.append((self.number(hi, lo, y, core), self.number(*to)))
        return lax.ppermute(x, AXES, pairs)

    def number(self, hi, lo, y, core):
        return (hi * 2 + lo) * self.cols + y * 2 + core

    def swap_lo(self, x):
        return self.send(x, lambda hi, lo, y, core: (hi, 1 - lo, y, core))

    def swap_core(self, x):
        return self.send(x, lambda hi, lo, y, core: (hi, lo, y, 1 - core))

    def swap_y(self, x, s):
        return self.send(x, lambda hi, lo, y, core: (hi, lo, y ^ s, core))

    def swap_hi(self, x, s):
        return self.send(x, lambda hi, lo, y, core: (hi ^ s, lo, y, core))


def after(x, *values):
    return lax.optimization_barrier((x, *values))[0]


def order_blocks(n):
    count = n // BLOCK
    lower = [(i, j) for i in range(count) for j in range(i + 1)]
    return lower, [(i, j) for i in range(count) for j in range(i + 1, count)]


def join(n, lookup):
    count = n // BLOCK
    zero = jnp.zeros((BLOCK, BLOCK), jnp.float32)
    return jnp.concatenate(
        [jnp.concatenate([lookup.get((i, j), zero) for j in range(count)], 1) for i in range(count)], 0
    )


def scatter(grid, tile):
    n = tile.shape[0]
    total = grid.rows * grid.cols
    parts = []
    for at in order_blocks(n):
        blocks = [tile[i * BLOCK : (i + 1) * BLOCK, j * BLOCK : (j + 1) * BLOCK] for i, j in at]
        parts.append(jnp.stack(blocks).reshape(total, -1, BLOCK))
    lower = parts[0].shape[1]
    got = lax.all_to_all(jnp.concatenate(parts, 1), AXES, 0, 0, tiled=True)
    corner, side, last = got[0, :lower], got[grid.cols], got[grid.cols + 1, :lower]
    return corner, jnp.concatenate([side, last], 0)


def gather(grid, part):
    spread = jnp.broadcast_to(part[None], (grid.rows * grid.cols, *part.shape))
    return lax.all_to_all(spread, AXES, 0, 0, tiled=True)


def unpack_lower(n, packed):
    lower, _ = order_blocks(n)
    packed = packed.reshape(len(lower), BLOCK, BLOCK)
    return join(n, {key: packed[k] for k, key in enumerate(lower)})


def unpack_sides(n, packed):
    lower, upper = order_blocks(n)
    rows = len(lower) * BLOCK // packed.shape[0]
    more = rows + len(upper) * BLOCK // packed.shape[0]
    low = packed[:, :rows].reshape(len(lower), BLOCK, BLOCK)
    high = packed[:, rows:more].reshape(len(upper), BLOCK, BLOCK)
    lookup = {key: low[k] for k, key in enumerate(lower)}
    lookup.update({key: high[k] for k, key in enumerate(upper)})
    return join(n, lookup), unpack_lower(n, packed[:, more:])


def split(x):
    high = x.astype(jnp.bfloat16)
    return high, (x - high.astype(jnp.float32)).astype(jnp.bfloat16)


def product(a, b, cb):
    def one(x, y):
        return lax.dot_general(x, y, (((1,), (cb,)), ((), ())), preferred_element_type=jnp.float32)

    return one(a[0], b[0]) + (one(a[0], b[1]) + one(a[1], b[0]))


def finish_kernel(shape, steps, opening, scalars, *refs):
    count, width, n = shape
    extra = count if opening else 0
    total = extra + len(steps)
    g_ref, l0_ref, l10_ref, l1_ref, w0_ref, w1_ref = refs[:6]
    refs = refs[6:]
    own = refs[: 2 * extra]
    refs = refs[2 * extra :]
    sets = [refs[4 * e : 4 * e + 4] for e in range(len(steps))]
    refs = refs[4 * len(steps) :]
    if not opening:
        _, rows_in = refs[0], refs[1:3]
        refs = refs[3:]
    out_ref = refs[0]
    rows_out = refs[1:3] if opening else ()
    refs = refs[3:] if opening else refs[1:]
    raw, rh, rl, ch, cl, keep, w0h, w0l, w1h, w1l, lh, ll, gbuf, obuf, rsem, gsem, osem, psem = refs
    core, same_lo, half, row0, row1, col = [scalars[k] for k in range(6)]

    def fetch(condition, ref, slot, panel):
        @pl.when(condition)
        def _():
            pltpu.make_async_copy(ref, raw.at[slot, panel], rsem.at[slot, panel]).start()

    for panel in range(2):
        for a in range(extra):
            fetch(core == panel, own[a], a, panel)
            fetch(core != panel, own[extra + a], a, panel)
    for e in range(len(steps)):
        straight, straight_got, crossed, crossed_got = sets[e]
        for panel in range(2):
            fetch((same_lo == 1) & (core == panel), straight, extra + e, panel)
            fetch((same_lo == 1) & (core != panel), straight_got, extra + e, panel)
            fetch((same_lo == 0) & (core == panel), crossed, extra + e, panel)
            fetch((same_lo == 0) & (core != panel), crossed_got, extra + e, panel)

    def column(e):
        slot = far = 0
        for at, (s, f) in enumerate(steps):
            slot = jnp.where(e == at, s, slot)
            far = jnp.where(e == at, f, far)
        return 2 * slot + jnp.where(far == 1, 1 - half, half)

    def place(k):
        return lax.rem(k, count), column(k // count)

    def g_copy(k, slot):
        a, t = place(k)
        return pltpu.make_async_copy(g_ref.at[a, t], gbuf.at[slot], gsem.at[slot])

    def o_copy(k, slot):
        a, t = place(k)
        return pltpu.make_async_copy(obuf.at[slot], out_ref.at[a, t], osem.at[slot])

    g_copy(0, 0).start()
    if not opening:
        row_copies = [
            pltpu.make_async_copy(rows_in[0], rh, psem.at[0]),
            pltpu.make_async_copy(rows_in[1], rl, psem.at[1]),
        ]
        for copy in row_copies:
            copy.start()
    w0h[...], w0l[...] = split(w0_ref[...])
    w1h[...], w1l[...] = split(w1_ref[...])
    lh[...], ll[...] = split(l10_ref[...])

    def solve(k, high, low, at, kept):
        pltpu.make_async_copy(sets[0][0], raw.at[k, 0], rsem.at[k, 0]).wait()
        p0 = product(split(raw[k, 0]), (w0h[...], w0l[...]), 1)
        pair = split(p0)
        high[at, 0] = pair[0]
        low[at, 0] = pair[1]
        pltpu.make_async_copy(sets[0][0], raw.at[k, 1], rsem.at[k, 1]).wait()
        left = raw[k, 1] - product(pair, (lh[...], ll[...]), 1)
        p1 = product(split(left), (w1h[...], w1l[...]), 1)
        high[at, 1], low[at, 1] = split(p1)
        if kept:
            keep[at, 0] = p0
            keep[at, 1] = p1

    def solve_row(k, carry):
        solve(k, rh, rl, k, True)
        return carry

    def solve_column(k, carry):
        solve(extra + k, ch, cl, k, False)
        return carry

    if opening:
        lax.fori_loop(0, extra, solve_row, 0)
        row_copies = [
            pltpu.make_async_copy(rh, rows_out[0], psem.at[0]),
            pltpu.make_async_copy(rl, rows_out[1], psem.at[1]),
        ]
        for copy in row_copies:
            copy.start()
    lax.fori_loop(0, len(steps), solve_column, 0)
    if not opening:
        for copy in row_copies:
            copy.wait()

    last = count * len(steps)

    def update(k, carry):
        slot = lax.rem(k, 2)
        a, t = place(k)
        e = k // count
        g_copy(k, slot).wait()

        @pl.when(k + 1 < last)
        def _():
            g_copy(k + 1, 1 - slot).start()

        @pl.when(k >= 2)
        def _():
            o_copy(k - 2, slot).wait()

        first_tile = (t == 0) & (col < 2) if opening else jnp.bool_(False)
        is_row0 = (a == 0) & (row0 == 1)
        is_row1 = (a == 0) & (row1 == 1)
        special = is_row0 | is_row1
        plain = jnp.logical_not(first_tile)

        @pl.when(plain & jnp.logical_not(special))
        def _():
            value = gbuf[slot]
            for panel in range(2):
                value = value - product((rh[a, panel], rl[a, panel]), (ch[e, panel], cl[e, panel]), 1)
            obuf[slot] = value

        @pl.when(plain & special)
        def _():
            obuf[slot] = jnp.zeros((n, n), jnp.float32)

        if opening:

            @pl.when(first_tile & jnp.logical_not(special))
            def _():
                obuf[slot] = keep[a, col]

            @pl.when(first_tile & is_row0)
            def _():
                obuf[slot] = jnp.where(col == 0, l0_ref[...], 0.0)

            @pl.when(first_tile & is_row1)
            def _():
                obuf[slot] = jnp.where(col == 0, l10_ref[...], l1_ref[...])

        o_copy(k, slot).start()
        return carry

    lax.fori_loop(0, last, update, 0)
    o_copy(last - 2, lax.rem(last, 2)).wait()
    o_copy(last - 1, lax.rem(last + 1, 2)).wait()
    if opening:
        for copy in row_copies:
            copy.wait()


def finish(grid, blocks, factors, steps, sets, own=None, before=None):
    count, width, n, _ = blocks.shape
    opening = before is None
    total = len(steps) + (count if opening else 0)
    scalars = jnp.stack(
        [
            grid.core,
            (grid.lo == grid.core).astype(jnp.int32),
            grid.hi // grid.ys,
            (grid.row == 0).astype(jnp.int32),
            (grid.row == 1).astype(jnp.int32),
            grid.col,
        ]
    ).astype(jnp.int32)
    inputs = [scalars, blocks, *factors]
    if opening:
        inputs += own
    for group in sets:
        inputs += group
    aliases = {}
    if not opening:
        aliases[len(inputs)] = 0
        inputs += before
    anywhere = pl.BlockSpec(memory_space=pl.ANY)
    vmem = pl.BlockSpec(memory_space=pltpu.VMEM)
    result = jax.ShapeDtypeStruct(blocks.shape, jnp.float32)
    panel = jax.ShapeDtypeStruct((count, 2, n, n), jnp.bfloat16)
    half = pltpu.VMEM((n, n), jnp.bfloat16)
    pair = pltpu.VMEM((2, n, n), jnp.float32)
    rows = pltpu.VMEM((count, 2, n, n), jnp.bfloat16)
    columns = pltpu.VMEM((len(steps), 2, n, n), jnp.bfloat16)
    return pl.pallas_call(
        functools.partial(finish_kernel, (count, width, n), steps, opening),
        out_shape=[result, panel, panel] if opening else [result],
        in_specs=[pl.BlockSpec(memory_space=pltpu.SMEM), anywhere] + [vmem] * 5 + [anywhere] * (len(inputs) - 7),
        out_specs=[anywhere] * (3 if opening else 1),
        scratch_shapes=[
            pltpu.VMEM((total, 2, n, n), jnp.float32),
            rows,
            rows,
            columns,
            columns,
            pltpu.VMEM((count, 2, n, n), jnp.float32),
            half,
            half,
            half,
            half,
            half,
            half,
            pair,
            pair,
            pltpu.SemaphoreType.DMA((total, 2)),
            pltpu.SemaphoreType.DMA((2,)),
            pltpu.SemaphoreType.DMA((2,)),
            pltpu.SemaphoreType.DMA((2,)),
        ],
        input_output_aliases=aliases,
        cost_estimate=pl.CostEstimate(flops=20_000_000_000, bytes_accessed=60_000_000, transcendentals=0),
        compiler_params=pltpu.CompilerParams(vmem_limit_bytes=58 * 1024 * 1024),
    )(*inputs)


def shards(gram_tiles):
    blocks = gram_tiles[:, 0, :, 0]
    grid = Grid()
    n = blocks.shape[-1]
    half = n // BLOCK // 2
    slots = range(blocks.shape[0])
    raw = [blocks[a, 0] for a in slots]

    def up(a):
        return [grid.send(raw[a], lambda hi, lo, y, core: (hi, lo, h, core) if y == 0 else None) for h in range(1, grid.ys)]

    def own_tile(a, got):
        tile = raw[a]
        for h in range(1, grid.ys):
            tile = jnp.where(grid.y == h, got[h - 1], tile)
        return tile

    def pair_start(tile):
        return [grid.swap_hi(tile, s) for s in range(1, grid.ys)]

    def pair_finish(tile, got):
        same = tile
        for s in range(1, grid.ys):
            same = jnp.where((grid.hi % grid.ys) ^ grid.y == s, got[s - 1], same)
        return same

    def cross(tile):
        if grid.ys == 2:
            return grid.send(tile, lambda hi, lo, y, core: (3 - hi, lo, y, core) if hi in (1, 2) else None)
        return grid.swap_hi(tile, grid.ys)

    def spread(tile):
        return grid.swap_hi(tile, 1) if grid.ys == 2 else tile

    def far_tile(middle, edge):
        return jnp.where((grid.hi == 1) | (grid.hi == 2), middle, edge) if grid.ys == 2 else middle

    part, sides = scatter(grid, raw[0])
    lifted = [up(a) for a in slots]
    corner = gather(grid, part)
    sides = gather(grid, after(sides, part))
    own = [own_tile(0, lifted[0]), None]
    paired = [pair_start(own[0]), None]
    x = after(unpack_lower(n, corner), own[0])

    a, l, w = call(functools.partial(open_kernel, half), n, (x,), 3)

    got, lift = lax.optimization_barrier((paired[0], lifted[1], a))[:2]
    near = [pair_finish(own[0], got), None]
    own[1] = own_tile(1, lift)
    middle = [cross(near[0]), None]
    paired[1] = pair_start(own[1])
    near_x = [grid.swap_lo(near[0]), None]
    a = after(a, near[0], own[1])
    l0, w0 = close(a, l, w)

    got, mid, sides = lax.optimization_barrier((paired[1], middle[0], sides, w0))[:3]
    middle[0] = mid
    near[1] = pair_finish(own[1], got)
    edge = [spread(middle[0]), None]
    middle[1] = cross(near[1])
    near_x[1] = grid.swap_lo(near[1])
    side0, side1 = unpack_sides(n, sides)
    side0 = after(side0, near[1])
    l10, a, l, w = call(functools.partial(corner_kernel, half), n, (side0, side1, w0), 4)

    eg, mid, nx = lax.optimization_barrier((edge[0], middle[1], near_x[0], a))[:3]
    edge[0], middle[1], near_x[0] = eg, mid, nx
    far = [far_tile(middle[0], edge[0]), None]
    edge[1] = spread(middle[1])
    far_x = [grid.swap_lo(far[0]), None]
    own_got = [grid.swap_core(after(own[k], a)) for k in slots]
    near_got = [grid.swap_core(after(near[k], a)) for k in slots]
    near_x_got = [grid.swap_core(near_x[0]), None]
    a = after(a, far[0])
    l1, w1 = close(a, l, w)

    eg, fx, nx = lax.optimization_barrier((edge[1], far_x[0], near_x[1], w1))[:3]
    edge[1], far_x[0], near_x[1] = eg, fx, nx
    far[1] = far_tile(middle[1], edge[1])
    far_x[1] = grid.swap_lo(far[1])
    far_got = [grid.swap_core(far[k]) for k in slots]
    near_x_got[1] = grid.swap_core(near_x[1])
    far_x_got = [grid.swap_core(far_x[0]), None]
    factors = (l0, l10, l1, w0, after(w1, far[1]))

    def groups(k, far_one):
        if far_one:
            return [far[k], far_got[k], far_x[k], far_x_got[k]]
        return [near[k], near_got[k], near_x[k], near_x_got[k]]

    steps = [(k, f) for k in slots for f in (0, 1)]
    head, rest = tuple(steps[:-1]), tuple(steps[-1:])
    done = finish(grid, blocks, factors, head, [groups(*step) for step in head], [*own, *own_got])
    far_x[1] = after(far_x[1], done[0])
    far_x_got[1] = grid.swap_core(far_x[1])
    blocks = finish(grid, blocks, factors, rest, [groups(*step) for step in rest], before=list(done))[0]
    return blocks[:, None, :, None]


def solution(mesh):
    placed = P(None, "row", None, "col", None, None)
    return jax.shard_map(shards, mesh=mesh, in_specs=(placed,), out_specs=placed, check_vma=False)
```

```python
import functools

import jax
import jax.numpy as jnp
from jax import lax
from jax.experimental import pallas as pl
from jax.experimental.pallas import tpu as pltpu
from jax.sharding import PartitionSpec as P

GROUP = 16
BLOCK = 128
AXES = ("row", "col")


def contract(a, b, ca, cb, precision=lax.Precision.HIGHEST):
    return lax.dot_general(
        a, b, (((ca,), (cb,)), ((), ())), precision=precision, preferred_element_type=jnp.float32
    )


def factor_block(s_ref, e_ref, u_ref):
    n = s_ref.shape[0]
    sub = lax.broadcasted_iota(jnp.int32, (GROUP, n), 0)
    lane = lax.broadcasted_iota(jnp.int32, (GROUP, n), 1)
    down = lax.broadcasted_iota(jnp.int32, (n, n), 0)
    across = lax.broadcasted_iota(jnp.int32, (n, n), 1)
    e_ref[...] = (down == across).astype(jnp.float32)
    for start in range(0, n, GROUP):
        stop = start + GROUP
        tall = s_ref[start:stop, :]
        unit = e_ref[start:stop, :]
        entry = {}
        for j in range(GROUP):
            for i in range(j, GROUP):
                entry[i, j] = jnp.broadcast_to(tall[j : j + 1, start + i : start + i + 1], (1, n))
        rows = [tall[t : t + 1, :] for t in range(GROUP)]
        units = [unit[t : t + 1, :] for t in range(GROUP)]
        for t in range(GROUP):
            scale = lax.rsqrt(entry[t, t])
            for i in range(t + 1, GROUP):
                entry[i, t] = entry[i, t] * scale
            rows[t] = rows[t] * scale
            units[t] = units[t] * scale
            for i in range(t + 1, GROUP):
                for j in range(t + 1, i + 1):
                    entry[i, j] = entry[i, j] - entry[i, t] * entry[j, t]
                rows[i] = rows[i] - entry[i, t] * rows[t]
                units[i] = units[i] - entry[i, t] * units[t]
        u = jnp.where(lane >= sub + start, jnp.concatenate(rows, 0), 0.0)
        v = jnp.concatenate(units, 0)
        u_ref[start:stop, :] = u
        e_ref[start:stop, :] = v
        if stop < n:
            s_ref[stop:, :] = s_ref[stop:, :] - contract(u, u, 0, 0)[stop:, :]
            e_ref[stop:, :] = e_ref[stop:, :] - contract(u, v, 0, 0)[stop:, :]


def eliminate(first, last, a_ref, l_ref, w_ref, s_ref, e_ref, u_ref):
    def step(k):
        begin = k * BLOCK
        end = begin + BLOCK
        at = slice(begin, end)
        later = slice(end, a_ref.shape[0])
        inverse = e_ref[...]
        l_ref[at, at] = u_ref[...].T
        w_ref[at, at] = inverse
        if begin > 0:
            solved = contract(inverse, w_ref[at, :begin], 1, 0)
            w_ref[at, :begin] = solved
        if end < a_ref.shape[0]:
            below = contract(a_ref[later, at], inverse, 1, 1)
            l_ref[later, at] = below
            a_ref[later, later] -= contract(below, below, 1, 1)
            w_ref[later, at] = -contract(below, inverse, 1, 0)
            if begin > 0:
                w_ref[later, :begin] -= contract(below, solved, 1, 0)

    def body(k, carry):
        at = pl.ds(pl.multiple_of(k * BLOCK, BLOCK), BLOCK)
        s_ref[...] = a_ref[at, at]
        factor_block(s_ref, e_ref, u_ref)
        for known in range(first, last):

            @pl.when(k == known)
            def _():
                step(known)

        return carry

    lax.fori_loop(first, last, body, 0)


def open_kernel(last, x_ref, rest_ref, l_ref, w_ref, a_ref, *scratch):
    a_ref[...] = x_ref[...]
    l_ref[...] = jnp.zeros_like(l_ref)
    w_ref[...] = jnp.zeros_like(w_ref)
    eliminate(0, last, a_ref, l_ref, w_ref, *scratch)
    rest_ref[...] = a_ref[last * BLOCK :, last * BLOCK :]


def corner_kernel(last, side_ref, x_ref, inverse_ref, p_ref, rest_ref, l_ref, w_ref, a_ref, *scratch):
    n = x_ref.shape[0]
    half = n // 2

    def solve(c, carry):
        at = pl.ds(pl.multiple_of(c * half, half), half)
        p_ref[:, at] = contract(side_ref[...], inverse_ref[at, :], 1, 1)
        return carry

    def subtract(c, carry):
        at = pl.ds(pl.multiple_of(c * half, half), half)
        a_ref[:, at] = x_ref[:, at] - contract(p_ref[...], p_ref[at, :], 1, 1)
        return carry

    lax.fori_loop(0, 2, solve, 0)
    lax.fori_loop(0, 2, subtract, 0)
    l_ref[...] = jnp.zeros_like(l_ref)
    w_ref[...] = jnp.zeros_like(w_ref)
    eliminate(0, last, a_ref, l_ref, w_ref, *scratch)
    rest_ref[...] = a_ref[last * BLOCK :, last * BLOCK :]


def close_kernel(first, last, rest_ref, l_in, w_in, l_ref, w_ref, a_ref, *scratch):
    a_ref[first * BLOCK :, first * BLOCK :] = rest_ref[...]
    l_ref[...] = l_in[...]
    w_ref[...] = w_in[...]
    eliminate(first, last, a_ref, l_ref, w_ref, *scratch)


def call(kernel, n, inputs, outputs):
    small = pltpu.VMEM((BLOCK, BLOCK), jnp.float32)
    space = pl.BlockSpec(memory_space=pltpu.VMEM)
    return pl.pallas_call(
        kernel,
        out_shape=[jax.ShapeDtypeStruct((size, size), jnp.float32) for size in outputs],
        in_specs=[space] * len(inputs),
        out_specs=[space] * len(outputs),
        scratch_shapes=[pltpu.VMEM((n, n), jnp.float32), small, small, small],
        cost_estimate=pl.CostEstimate(flops=20_000_000_000, bytes_accessed=60_000_000, transcendentals=0),
    )(*inputs)


def halfway(n):
    return n // BLOCK // 2


def left(n):
    return n - halfway(n) * BLOCK


def factor_open(x):
    n = x.shape[0]
    return call(functools.partial(open_kernel, halfway(n)), n, (x,), (left(n), n, n))


def factor_corner(side, x, inverse):
    n = x.shape[0]
    return call(functools.partial(corner_kernel, halfway(n)), n, (side, x, inverse), (n, left(n), n, n))


def factor_close(rest, l, w):
    n = l.shape[0]
    return call(functools.partial(close_kernel, halfway(n), n // BLOCK), n, (rest, l, w), (n, n))


class Grid:
    def __init__(self):
        self.rows = lax.axis_size("row")
        self.cols = lax.axis_size("col")
        self.his = self.rows // 2
        self.ys = self.cols // 2
        row = lax.axis_index("row")
        col = lax.axis_index("col")
        self.row, self.col = row, col
        self.hi, self.lo, self.y, self.core = row // 2, row % 2, col // 2, col % 2

    def send(self, x, target):
        pairs = []
        for hi in range(self.his):
            for lo in range(2):
                for y in range(self.ys):
                    for core in range(2):
                        to = target(hi, lo, y, core)
                        if to is not None:
                            pairs.append((self.number(hi, lo, y, core), self.number(*to)))
        return lax.ppermute(x, AXES, pairs)

    def number(self, hi, lo, y, core):
        return (hi * 2 + lo) * self.cols + y * 2 + core

    def swap_lo(self, x):
        return self.send(x, lambda hi, lo, y, core: (hi, 1 - lo, y, core))

    def swap_core(self, x):
        return self.send(x, lambda hi, lo, y, core: (hi, lo, y, 1 - core))

    def swap_y(self, x, s):
        return self.send(x, lambda hi, lo, y, core: (hi, lo, y ^ s, core))

    def swap_hi(self, x, s):
        return self.send(x, lambda hi, lo, y, core: (hi ^ s, lo, y, core))


def after(x, *values):
    return lax.optimization_barrier((x, *values))[0]


def order_blocks(n):
    count = n // BLOCK
    lower = [(i, j) for i in range(count) for j in range(i + 1)]
    return lower, [(i, j) for i in range(count) for j in range(i + 1, count)]


def join(n, lookup):
    count = n // BLOCK
    zero = jnp.zeros((BLOCK, BLOCK), jnp.float32)
    return jnp.concatenate(
        [jnp.concatenate([lookup.get((i, j), zero) for j in range(count)], 1) for i in range(count)], 0
    )


def scatter(grid, tile):
    n = tile.shape[0]
    total = grid.rows * grid.cols
    parts = []
    for at in order_blocks(n):
        blocks = [tile[i * BLOCK : (i + 1) * BLOCK, j * BLOCK : (j + 1) * BLOCK] for i, j in at]
        parts.append(jnp.stack(blocks).reshape(total, -1, BLOCK))
    lower = parts[0].shape[1]
    got = lax.all_to_all(jnp.concatenate(parts, 1), AXES, 0, 0, tiled=True)
    corner, side, last = got[0, :lower], got[grid.cols], got[grid.cols + 1, :lower]
    return corner, jnp.concatenate([side, last], 0)


def gather(grid, part):
    spread = jnp.broadcast_to(part[None], (grid.rows * grid.cols, *part.shape))
    return lax.all_to_all(spread, AXES, 0, 0, tiled=True)


def unpack_lower(n, packed):
    lower, _ = order_blocks(n)
    packed = packed.reshape(len(lower), BLOCK, BLOCK)
    return join(n, {key: packed[k] for k, key in enumerate(lower)})


def unpack_sides(n, packed):
    lower, upper = order_blocks(n)
    rows = len(lower) * BLOCK // packed.shape[0]
    more = rows + len(upper) * BLOCK // packed.shape[0]
    low = packed[:, :rows].reshape(len(lower), BLOCK, BLOCK)
    high = packed[:, rows:more].reshape(len(upper), BLOCK, BLOCK)
    lookup = {key: low[k] for k, key in enumerate(lower)}
    lookup.update({key: high[k] for k, key in enumerate(upper)})
    return join(n, lookup), unpack_lower(n, packed[:, more:])


def split(x):
    high = x.astype(jnp.bfloat16)
    return high, (x - high.astype(jnp.float32)).astype(jnp.bfloat16)


def product(a, b, cb):
    def one(x, y):
        return lax.dot_general(x, y, (((1,), (cb,)), ((), ())), preferred_element_type=jnp.float32)

    return one(a[0], b[0]) + (one(a[0], b[1]) + one(a[1], b[0]))


def finish_kernel(shape, steps, opening, scalars, *refs):
    count, width, n = shape
    extra = count if opening else 0
    total = extra + len(steps)
    g_ref, l0_ref, l10_ref, l1_ref, w0_ref, w1_ref = refs[:6]
    refs = refs[6:]
    own = refs[: 2 * extra]
    refs = refs[2 * extra :]
    sets = [refs[4 * e : 4 * e + 4] for e in range(len(steps))]
    refs = refs[4 * len(steps) :]
    if not opening:
        _, rows_in = refs[0], refs[1:3]
        refs = refs[3:]
    out_ref = refs[0]
    rows_out = refs[1:3] if opening else ()
    refs = refs[3:] if opening else refs[1:]
    raw, high, low, keep, w0h, w0l, w1h, w1l, lh, ll, gbuf, obuf, rsem, gsem, osem, psem = refs
    core, same_lo, half, row0, row1, col = [scalars[k] for k in range(6)]

    def fetch(condition, ref, slot, panel):
        @pl.when(condition)
        def _():
            pltpu.make_async_copy(ref, raw.at[slot, panel], rsem.at[slot, panel]).start()

    for panel in range(2):
        for a in range(extra):
            fetch(core == panel, own[a], a, panel)
            fetch(core != panel, own[extra + a], a, panel)
    for e in range(len(steps)):
        straight, straight_got, crossed, crossed_got = sets[e]
        for panel in range(2):
            fetch((same_lo == 1) & (core == panel), straight, extra + e, panel)
            fetch((same_lo == 1) & (core != panel), straight_got, extra + e, panel)
            fetch((same_lo == 0) & (core == panel), crossed, extra + e, panel)
            fetch((same_lo == 0) & (core != panel), crossed_got, extra + e, panel)

    def column(e):
        slot = far = 0
        for at, (s, f) in enumerate(steps):
            slot = jnp.where(e == at, s, slot)
            far = jnp.where(e == at, f, far)
        return 2 * slot + jnp.where(far == 1, 1 - half, half)

    def place(k):
        return lax.rem(k, count), column(k // count)

    def g_copy(k, slot):
        a, t = place(k)
        return pltpu.make_async_copy(g_ref.at[a, t], gbuf.at[slot], gsem.at[slot])

    def o_copy(k, slot):
        a, t = place(k)
        return pltpu.make_async_copy(obuf.at[slot], out_ref.at[a, t], osem.at[slot])

    g_copy(0, 0).start()
    held = (high.at[:count], low.at[:count])
    if not opening:
        row_copies = [pltpu.make_async_copy(rows_in[k], held[k], psem.at[k]) for k in range(2)]
        for copy in row_copies:
            copy.start()
    w0h[...], w0l[...] = split(w0_ref[...])
    w1h[...], w1l[...] = split(w1_ref[...])
    lh[...], ll[...] = split(l10_ref[...])

    mid = n // 2

    def times_lower(x, yh, yl):
        head = product((x[0][:, :mid], x[1][:, :mid]), (yh[:mid, :mid], yl[:mid, :mid]), 1)
        return jnp.concatenate([head, product(x, (yh[mid:, :], yl[mid:, :]), 1)], 1)

    def solve(k, carry):
        at = k if opening else k + count
        pltpu.make_async_copy(sets[0][0], raw.at[k, 0], rsem.at[k, 0]).wait()
        p0 = times_lower(split(raw[k, 0]), w0h, w0l)
        high[at, 0], low[at, 0] = split(p0)
        pltpu.make_async_copy(sets[0][0], raw.at[k, 1], rsem.at[k, 1]).wait()

        def strip(c, carry):
            part = pl.ds(pl.multiple_of(c * mid, mid), mid)
            whole = (high[at, 0], low[at, 0])
            raw[k, 1, :, part] = raw[k, 1, :, part] - product(whole, (lh[part, :], ll[part, :]), 1)
            return carry

        lax.fori_loop(0, 2, strip, 0)
        p1 = times_lower(split(raw[k, 1]), w1h, w1l)
        high[at, 1], low[at, 1] = split(p1)
        if opening:

            @pl.when(k < count)
            def _():
                keep[k, 0] = p0
                keep[k, 1] = p1

        return carry

    lax.fori_loop(0, total, solve, 0)
    if opening:
        row_copies = [pltpu.make_async_copy(held[k], rows_out[k], psem.at[k]) for k in range(2)]
        for copy in row_copies:
            copy.start()
    else:
        for copy in row_copies:
            copy.wait()

    last = count * len(steps)

    def update(k, carry):
        slot = lax.rem(k, 2)
        a, t = place(k)
        e = k // count
        g_copy(k, slot).wait()

        @pl.when(k + 1 < last)
        def _():
            g_copy(k + 1, 1 - slot).start()

        @pl.when(k >= 2)
        def _():
            o_copy(k - 2, slot).wait()

        first_tile = (t == 0) & (col < 2) if opening else jnp.bool_(False)
        is_row0 = (a == 0) & (row0 == 1)
        is_row1 = (a == 0) & (row1 == 1)
        special = is_row0 | is_row1
        plain = jnp.logical_not(first_tile)

        @pl.when(plain & jnp.logical_not(special))
        def _():
            def strip(c, carry):
                at = pl.ds(pl.multiple_of(c * mid, mid), mid)
                value = gbuf[slot, :, at]
                for panel in range(2):
                    column_part = (high[count + e, panel, at, :], low[count + e, panel, at, :])
                    value = value - product((high[a, panel], low[a, panel]), column_part, 1)
                obuf[slot, :, at] = value
                return carry

            lax.fori_loop(0, 2, strip, 0)

        @pl.when(plain & special)
        def _():
            obuf[slot] = jnp.zeros((n, n), jnp.float32)

        if opening:

            @pl.when(first_tile & jnp.logical_not(special))
            def _():
                obuf[slot] = keep[a, col]

            @pl.when(first_tile & is_row0)
            def _():
                obuf[slot] = jnp.where(col == 0, l0_ref[...], 0.0)

            @pl.when(first_tile & is_row1)
            def _():
                obuf[slot] = jnp.where(col == 0, l10_ref[...], l1_ref[...])

        o_copy(k, slot).start()
        return carry

    lax.fori_loop(0, last, update, 0)
    o_copy(last - 2, lax.rem(last, 2)).wait()
    o_copy(last - 1, lax.rem(last + 1, 2)).wait()
    if opening:
        for copy in row_copies:
            copy.wait()


def finish(grid, blocks, factors, steps, sets, own=None, before=None):
    count, width, n, _ = blocks.shape
    opening = before is None
    total = len(steps) + (count if opening else 0)
    scalars = jnp.stack(
        [
            grid.core,
            (grid.lo == grid.core).astype(jnp.int32),
            grid.hi // grid.ys,
            (grid.row == 0).astype(jnp.int32),
            (grid.row == 1).astype(jnp.int32),
            grid.col,
        ]
    ).astype(jnp.int32)
    inputs = [scalars, blocks, *factors]
    if opening:
        inputs += own
    for group in sets:
        inputs += group
    aliases = {}
    if not opening:
        aliases[len(inputs)] = 0
        inputs += before
    anywhere = pl.BlockSpec(memory_space=pl.ANY)
    vmem = pl.BlockSpec(memory_space=pltpu.VMEM)
    result = jax.ShapeDtypeStruct(blocks.shape, jnp.float32)
    panel = jax.ShapeDtypeStruct((count, 2, n, n), jnp.bfloat16)
    half = pltpu.VMEM((n, n), jnp.bfloat16)
    pair = pltpu.VMEM((2, n, n), jnp.float32)
    panels = pltpu.VMEM((count + len(steps), 2, n, n), jnp.bfloat16)
    return pl.pallas_call(
        functools.partial(finish_kernel, (count, width, n), steps, opening),
        out_shape=[result, panel, panel] if opening else [result],
        in_specs=[pl.BlockSpec(memory_space=pltpu.SMEM), anywhere] + [vmem] * 5 + [anywhere] * (len(inputs) - 7),
        out_specs=[anywhere] * (3 if opening else 1),
        scratch_shapes=[
            pltpu.VMEM((total, 2, n, n), jnp.float32),
            panels,
            panels,
            pltpu.VMEM((count, 2, n, n), jnp.float32),
            half,
            half,
            half,
            half,
            half,
            half,
            pair,
            pair,
            pltpu.SemaphoreType.DMA((total, 2)),
            pltpu.SemaphoreType.DMA((2,)),
            pltpu.SemaphoreType.DMA((2,)),
            pltpu.SemaphoreType.DMA((2,)),
        ],
        input_output_aliases=aliases,
        cost_estimate=pl.CostEstimate(flops=20_000_000_000, bytes_accessed=60_000_000, transcendentals=0),
        compiler_params=pltpu.CompilerParams(vmem_limit_bytes=58 * 1024 * 1024),
    )(*inputs)


def shards(gram_tiles):
    blocks = gram_tiles[:, 0, :, 0]
    grid = Grid()
    n = blocks.shape[-1]
    slots = range(blocks.shape[0])
    raw = [blocks[a, 0] for a in slots]

    def up(a):
        return [grid.send(raw[a], lambda hi, lo, y, core: (hi, lo, h, core) if y == 0 else None) for h in range(1, grid.ys)]

    def own_tile(a, got):
        tile = raw[a]
        for h in range(1, grid.ys):
            tile = jnp.where(grid.y == h, got[h - 1], tile)
        return tile

    def pair_start(tile):
        return [grid.swap_hi(tile, s) for s in range(1, grid.ys)]

    def pair_finish(tile, got):
        same = tile
        for s in range(1, grid.ys):
            same = jnp.where((grid.hi % grid.ys) ^ grid.y == s, got[s - 1], same)
        return same

    def cross(tile):
        if grid.ys == 2:
            return grid.send(tile, lambda hi, lo, y, core: (3 - hi, lo, y, core) if hi in (1, 2) else None)
        return grid.swap_hi(tile, grid.ys)

    def spread(tile):
        return grid.swap_hi(tile, 1) if grid.ys == 2 else tile

    def far_tile(middle, edge):
        return jnp.where((grid.hi == 1) | (grid.hi == 2), middle, edge) if grid.ys == 2 else middle

    part, sides = scatter(grid, raw[0])
    lifted = [up(a) for a in slots]
    corner = gather(grid, part)
    sides = gather(grid, after(sides, part))
    own = [own_tile(0, lifted[0]), None]
    paired = [pair_start(own[0]), None]
    x = after(unpack_lower(n, corner), own[0])

    a, l, w = factor_open(x)

    got, lift = lax.optimization_barrier((paired[0], lifted[1], a))[:2]
    near = [pair_finish(own[0], got), None]
    own[1] = own_tile(1, lift)
    middle = [cross(near[0]), None]
    paired[1] = pair_start(own[1])
    near_x = [grid.swap_lo(near[0]), None]
    a = after(a, near[0], own[1])
    l0, w0 = factor_close(a, l, w)

    got, mid, sides = lax.optimization_barrier((paired[1], middle[0], sides, w0))[:3]
    middle[0] = mid
    near[1] = pair_finish(own[1], got)
    edge = [spread(middle[0]), None]
    middle[1] = cross(near[1])
    near_x[1] = grid.swap_lo(near[1])
    side0, side1 = unpack_sides(n, sides)
    side0 = after(side0, near[1])
    l10, a, l, w = factor_corner(side0, side1, w0)

    eg, mid, nx = lax.optimization_barrier((edge[0], middle[1], near_x[0], a))[:3]
    edge[0], middle[1], near_x[0] = eg, mid, nx
    far = [far_tile(middle[0], edge[0]), None]
    edge[1] = spread(middle[1])
    far_x = [grid.swap_lo(far[0]), None]
    own_got = [grid.swap_core(after(own[k], a)) for k in slots]
    near_got = [grid.swap_core(after(near[k], a)) for k in slots]
    near_x_got = [grid.swap_core(near_x[0]), None]
    a = after(a, far[0])
    l1, w1 = factor_close(a, l, w)

    eg, fx, nx = lax.optimization_barrier((edge[1], far_x[0], near_x[1], w1))[:3]
    edge[1], far_x[0], near_x[1] = eg, fx, nx
    far[1] = far_tile(middle[1], edge[1])
    far_x[1] = grid.swap_lo(far[1])
    far_got = [grid.swap_core(far[k]) for k in slots]
    near_x_got[1] = grid.swap_core(near_x[1])
    far_x_got = [grid.swap_core(far_x[0]), None]
    factors = (l0, l10, l1, w0, after(w1, far[1]))

    def groups(k, far_one):
        if far_one:
            return [far[k], far_got[k], far_x[k], far_x_got[k]]
        return [near[k], near_got[k], near_x[k], near_x_got[k]]

    steps = [(k, f) for k in slots for f in (0, 1)]
    head, rest = tuple(steps[:-1]), tuple(steps[-1:])
    done = finish(grid, blocks, factors, head, [groups(*step) for step in head], [*own, *own_got])
    far_x[1] = after(far_x[1], done[0])
    far_x_got[1] = grid.swap_core(far_x[1])
    blocks = finish(grid, blocks, factors, rest, [groups(*step) for step in rest], before=list(done))[0]
    return blocks[:, None, :, None]


def solution(mesh):
    placed = P(None, "row", None, "col", None, None)
    return jax.shard_map(shards, mesh=mesh, in_specs=(placed,), out_specs=placed, check_vma=False)
```

```python
import functools

import jax
import jax.numpy as jnp
from jax import lax
from jax.experimental import pallas as pl
from jax.experimental.pallas import tpu as pltpu
from jax.sharding import PartitionSpec as P

GROUP = 8
BLOCK = 128
AXES = ("row", "y", "core")


def contract(a, b, ca, cb, precision=lax.Precision.HIGHEST):
    return lax.dot_general(
        a, b, (((ca,), (cb,)), ((), ())), precision=precision, preferred_element_type=jnp.float32
    )


def factor_block(s_ref, e_ref, u_ref):
    n = s_ref.shape[0]
    sub = lax.broadcasted_iota(jnp.int32, (GROUP, n), 0)
    lane = lax.broadcasted_iota(jnp.int32, (GROUP, n), 1)
    down = lax.broadcasted_iota(jnp.int32, (n, n), 0)
    across = lax.broadcasted_iota(jnp.int32, (n, n), 1)
    e_ref[...] = (down == across).astype(jnp.float32)
    for start in range(0, n, GROUP):
        stop = start + GROUP
        tall = s_ref[start:stop, :]
        unit = e_ref[start:stop, :]
        entry = {}
        for j in range(GROUP):
            for i in range(j, GROUP):
                entry[i, j] = jnp.broadcast_to(tall[j : j + 1, start + i : start + i + 1], (1, n))
        rows = [tall[t : t + 1, :] for t in range(GROUP)]
        units = [unit[t : t + 1, :] for t in range(GROUP)]
        for t in range(GROUP):
            scale = lax.rsqrt(entry[t, t])
            for i in range(t + 1, GROUP):
                entry[i, t] = entry[i, t] * scale
            rows[t] = rows[t] * scale
            units[t] = units[t] * scale
            for i in range(t + 1, GROUP):
                for j in range(t + 1, i + 1):
                    entry[i, j] = entry[i, j] - entry[i, t] * entry[j, t]
                rows[i] = rows[i] - entry[i, t] * rows[t]
                units[i] = units[i] - entry[i, t] * units[t]
        u = jnp.where(lane >= sub + start, jnp.concatenate(rows, 0), 0.0)
        v = jnp.concatenate(units, 0)
        u_ref[start:stop, :] = u
        e_ref[start:stop, :] = v
        if stop < n:
            s_ref[stop:, :] = s_ref[stop:, :] - contract(u, u, 0, 0)[stop:, :]
            e_ref[stop:, :] = e_ref[stop:, :] - contract(u, v, 0, 0)[stop:, :]


def eliminate(first, last, a_ref, l_ref, w_ref, s_ref, e_ref, u_ref):
    def step(k):
        begin = k * BLOCK
        end = begin + BLOCK
        at = slice(begin, end)
        later = slice(end, a_ref.shape[0])
        inverse = e_ref[...]
        l_ref[at, at] = u_ref[...].T
        w_ref[at, at] = inverse
        if begin > 0:
            solved = contract(inverse, w_ref[at, :begin], 1, 0)
            w_ref[at, :begin] = solved
        if end < a_ref.shape[0]:
            below = contract(a_ref[later, at], inverse, 1, 1)
            l_ref[later, at] = below
            a_ref[later, later] -= contract(below, below, 1, 1)
            w_ref[later, at] = -contract(below, inverse, 1, 0)
            if begin > 0:
                w_ref[later, :begin] -= contract(below, solved, 1, 0)

    def body(k, carry):
        at = pl.ds(pl.multiple_of(k * BLOCK, BLOCK), BLOCK)
        s_ref[...] = a_ref[at, at]
        factor_block(s_ref, e_ref, u_ref)
        for known in range(first, last):

            @pl.when(k == known)
            def _():
                step(known)

        return carry

    lax.fori_loop(first, last, body, 0)


def open_kernel(last, x_ref, rest_ref, l_ref, w_ref, a_ref, *scratch):
    a_ref[...] = x_ref[...]
    l_ref[...] = jnp.zeros_like(l_ref)
    w_ref[...] = jnp.zeros_like(w_ref)
    eliminate(0, last, a_ref, l_ref, w_ref, *scratch)
    rest_ref[...] = a_ref[last * BLOCK :, last * BLOCK :]


def corner_kernel(last, side_ref, x_ref, inverse_ref, p_ref, rest_ref, l_ref, w_ref, a_ref, *scratch):
    n = x_ref.shape[0]
    half = n // 2

    def solve(c, carry):
        at = pl.ds(pl.multiple_of(c * half, half), half)
        p_ref[:, at] = contract(side_ref[...], inverse_ref[at, :], 1, 1)
        return carry

    def subtract(c, carry):
        at = pl.ds(pl.multiple_of(c * half, half), half)
        a_ref[:, at] = x_ref[:, at] - contract(p_ref[...], p_ref[at, :], 1, 1)
        return carry

    lax.fori_loop(0, 2, solve, 0)
    lax.fori_loop(0, 2, subtract, 0)
    l_ref[...] = jnp.zeros_like(l_ref)
    w_ref[...] = jnp.zeros_like(w_ref)
    eliminate(0, last, a_ref, l_ref, w_ref, *scratch)
    rest_ref[...] = a_ref[last * BLOCK :, last * BLOCK :]


def close_kernel(first, last, rest_ref, l_in, w_in, l_ref, w_ref, a_ref, *scratch):
    a_ref[first * BLOCK :, first * BLOCK :] = rest_ref[...]
    l_ref[...] = l_in[...]
    w_ref[...] = w_in[...]
    eliminate(first, last, a_ref, l_ref, w_ref, *scratch)


def call(kernel, n, inputs, outputs):
    small = pltpu.VMEM((BLOCK, BLOCK), jnp.float32)
    space = pl.BlockSpec(memory_space=pltpu.VMEM)
    return pl.pallas_call(
        kernel,
        out_shape=[jax.ShapeDtypeStruct((size, size), jnp.float32) for size in outputs],
        in_specs=[space] * len(inputs),
        out_specs=[space] * len(outputs),
        scratch_shapes=[pltpu.VMEM((n, n), jnp.float32), small, small, small],
        cost_estimate=pl.CostEstimate(flops=20_000_000_000, bytes_accessed=60_000_000, transcendentals=0),
    )(*inputs)


def halfway(n):
    return n // BLOCK // 2


def left(n):
    return n - halfway(n) * BLOCK


def factor_open(x):
    n = x.shape[0]
    return call(functools.partial(open_kernel, halfway(n)), n, (x,), (left(n), n, n))


def factor_corner(side, x, inverse):
    n = x.shape[0]
    return call(functools.partial(corner_kernel, halfway(n)), n, (side, x, inverse), (n, left(n), n, n))


def factor_close(rest, l, w):
    n = l.shape[0]
    return call(functools.partial(close_kernel, halfway(n), n // BLOCK), n, (rest, l, w), (n, n))


class Grid:
    def __init__(self):
        self.rows = lax.axis_size("row")
        self.ys = lax.axis_size("y")
        self.cols = self.ys * 2
        self.his = self.rows // 2
        self.row, self.y, self.core = [lax.axis_index(axis) for axis in AXES]
        self.col = self.y * 2 + self.core
        self.hi, self.lo = self.row // 2, self.row % 2

    def send(self, x, target):
        pairs = []
        for hi in range(self.his):
            for lo in range(2):
                for y in range(self.ys):
                    for core in range(2):
                        to = target(hi, lo, y, core)
                        if to is not None:
                            pairs.append((self.number(hi, lo, y, core), self.number(*to)))
        return lax.ppermute(x, AXES, pairs)

    def number(self, hi, lo, y, core):
        return (hi * 2 + lo) * self.cols + y * 2 + core

    def swap_lo(self, x):
        return self.send(x, lambda hi, lo, y, core: (hi, 1 - lo, y, core))

    def swap_core(self, x):
        return self.send(x, lambda hi, lo, y, core: (hi, lo, y, 1 - core))

    def swap_y(self, x, s):
        return self.send(x, lambda hi, lo, y, core: (hi, lo, y ^ s, core))

    def swap_hi(self, x, s):
        return self.send(x, lambda hi, lo, y, core: (hi ^ s, lo, y, core))


def after(x, *values):
    return lax.optimization_barrier((x, *values))[0]


def order_blocks(n):
    count = n // BLOCK
    lower = [(i, j) for i in range(count) for j in range(i + 1)]
    return lower, [(i, j) for i in range(count) for j in range(i + 1, count)]


def join(n, lookup):
    count = n // BLOCK
    zero = jnp.zeros((BLOCK, BLOCK), jnp.float32)
    return jnp.concatenate(
        [jnp.concatenate([lookup.get((i, j), zero) for j in range(count)], 1) for i in range(count)], 0
    )


def scatter(grid, tile):
    n = tile.shape[0]
    total = grid.rows * grid.cols
    parts = []
    for at in order_blocks(n):
        blocks = [tile[i * BLOCK : (i + 1) * BLOCK, j * BLOCK : (j + 1) * BLOCK] for i, j in at]
        parts.append(jnp.stack(blocks).reshape(total, -1, BLOCK))
    lower = parts[0].shape[1]
    got = lax.all_to_all(jnp.concatenate(parts, 1), AXES, 0, 0, tiled=True)
    corner, side, last = got[0, :lower], got[grid.cols], got[grid.cols + 1, :lower]
    return corner, jnp.concatenate([side, last], 0)


def gather(grid, part):
    spread = jnp.broadcast_to(part[None], (grid.rows * grid.ys, *part.shape))
    mine = lax.all_to_all(spread, ("row", "y"), 0, 0, tiled=True)
    return mine, grid.swap_core(mine)


def merge(grid, mine, other):
    even = grid.core == 0
    whole = jnp.stack([jnp.where(even, mine, other), jnp.where(even, other, mine)], 1)
    return whole.reshape(-1, *mine.shape[1:])


def unpack_lower(n, packed):
    lower, _ = order_blocks(n)
    packed = packed.reshape(len(lower), BLOCK, BLOCK)
    return join(n, {key: packed[k] for k, key in enumerate(lower)})


def unpack_sides(n, packed):
    lower, upper = order_blocks(n)
    rows = len(lower) * BLOCK // packed.shape[0]
    more = rows + len(upper) * BLOCK // packed.shape[0]
    low = packed[:, :rows].reshape(len(lower), BLOCK, BLOCK)
    high = packed[:, rows:more].reshape(len(upper), BLOCK, BLOCK)
    lookup = {key: low[k] for k, key in enumerate(lower)}
    lookup.update({key: high[k] for k, key in enumerate(upper)})
    return join(n, lookup), unpack_lower(n, packed[:, more:])


def split(x):
    high = x.astype(jnp.bfloat16)
    return high, (x - high.astype(jnp.float32)).astype(jnp.bfloat16)


def product(a, b, cb):
    def one(x, y):
        return lax.dot_general(x, y, (((1,), (cb,)), ((), ())), preferred_element_type=jnp.float32)

    return one(a[0], b[0]) + (one(a[0], b[1]) + one(a[1], b[0]))


def finish_kernel(shape, steps, opening, scalars, *refs):
    count, width, n = shape
    extra = count if opening else 0
    total = extra + len(steps)
    g_ref, l0_ref, l10_ref, l1_ref, w0_ref, w1_ref = refs[:6]
    refs = refs[6:]
    own = refs[: 2 * extra]
    refs = refs[2 * extra :]
    sets = [refs[4 * e : 4 * e + 4] for e in range(len(steps))]
    refs = refs[4 * len(steps) :]
    if not opening:
        _, rows_in = refs[0], refs[1:3]
        refs = refs[3:]
    out_ref = refs[0]
    rows_out = refs[1:3] if opening else ()
    refs = refs[3:] if opening else refs[1:]
    raw, high, low, keep, w0h, w0l, w1h, w1l, lh, ll, gbuf, obuf, rsem, gsem, osem, psem = refs
    core, same_lo, half, row0, row1, col = [scalars[k] for k in range(6)]

    def fetch(condition, ref, slot, panel):
        @pl.when(condition)
        def _():
            pltpu.make_async_copy(ref, raw.at[slot, panel], rsem.at[slot, panel]).start()

    for panel in range(2):
        for a in range(extra):
            fetch(core == panel, own[a], a, panel)
            fetch(core != panel, own[extra + a], a, panel)
    for e in range(len(steps)):
        straight, straight_got, crossed, crossed_got = sets[e]
        for panel in range(2):
            fetch((same_lo == 1) & (core == panel), straight, extra + e, panel)
            fetch((same_lo == 1) & (core != panel), straight_got, extra + e, panel)
            fetch((same_lo == 0) & (core == panel), crossed, extra + e, panel)
            fetch((same_lo == 0) & (core != panel), crossed_got, extra + e, panel)

    def column(e):
        slot = far = 0
        for at, (s, f) in enumerate(steps):
            slot = jnp.where(e == at, s, slot)
            far = jnp.where(e == at, f, far)
        return 2 * slot + jnp.where(far == 1, 1 - half, half)

    def place(k):
        return lax.rem(k, count), column(k // count)

    def g_copy(k, slot):
        a, t = place(k)
        return pltpu.make_async_copy(g_ref.at[a, t], gbuf.at[slot], gsem.at[slot])

    def o_copy(k, slot):
        a, t = place(k)
        return pltpu.make_async_copy(obuf.at[slot], out_ref.at[a, t], osem.at[slot])

    g_copy(0, 0).start()
    held = (high.at[:count], low.at[:count])
    if not opening:
        row_copies = [pltpu.make_async_copy(rows_in[k], held[k], psem.at[k]) for k in range(2)]
        for copy in row_copies:
            copy.start()
    w0h[...], w0l[...] = split(w0_ref[...])
    w1h[...], w1l[...] = split(w1_ref[...])
    lh[...], ll[...] = split(l10_ref[...])

    mid = n // 2

    def times_lower(x, yh, yl):
        head = product((x[0][:, :mid], x[1][:, :mid]), (yh[:mid, :mid], yl[:mid, :mid]), 1)
        return jnp.concatenate([head, product(x, (yh[mid:, :], yl[mid:, :]), 1)], 1)

    def solve(k, carry):
        at = k if opening else k + count
        pltpu.make_async_copy(sets[0][0], raw.at[k, 0], rsem.at[k, 0]).wait()
        p0 = times_lower(split(raw[k, 0]), w0h, w0l)
        high[at, 0], low[at, 0] = split(p0)
        pltpu.make_async_copy(sets[0][0], raw.at[k, 1], rsem.at[k, 1]).wait()

        def strip(c, carry):
            part = pl.ds(pl.multiple_of(c * mid, mid), mid)
            whole = (high[at, 0], low[at, 0])
            raw[k, 1, :, part] = raw[k, 1, :, part] - product(whole, (lh[part, :], ll[part, :]), 1)
            return carry

        lax.fori_loop(0, 2, strip, 0)
        p1 = times_lower(split(raw[k, 1]), w1h, w1l)
        high[at, 1], low[at, 1] = split(p1)
        if opening:

            @pl.when(k < count)
            def _():
                keep[k, 0] = p0
                keep[k, 1] = p1

        return carry

    lax.fori_loop(0, total, solve, 0)
    if opening:
        row_copies = [pltpu.make_async_copy(held[k], rows_out[k], psem.at[k]) for k in range(2)]
        for copy in row_copies:
            copy.start()
    else:
        for copy in row_copies:
            copy.wait()

    last = count * len(steps)

    def update(k, carry):
        slot = lax.rem(k, 2)
        a, t = place(k)
        e = k // count
        g_copy(k, slot).wait()

        @pl.when(k + 1 < last)
        def _():
            g_copy(k + 1, 1 - slot).start()

        @pl.when(k >= 2)
        def _():
            o_copy(k - 2, slot).wait()

        first_tile = (t == 0) & (col < 2) if opening else jnp.bool_(False)
        is_row0 = (a == 0) & (row0 == 1)
        is_row1 = (a == 0) & (row1 == 1)
        special = is_row0 | is_row1
        plain = jnp.logical_not(first_tile)

        @pl.when(plain & jnp.logical_not(special))
        def _():
            def strip(c, carry):
                at = pl.ds(pl.multiple_of(c * mid, mid), mid)
                value = gbuf[slot, :, at]
                for panel in range(2):
                    column_part = (high[count + e, panel, at, :], low[count + e, panel, at, :])
                    value = value - product((high[a, panel], low[a, panel]), column_part, 1)
                obuf[slot, :, at] = value
                return carry

            lax.fori_loop(0, 2, strip, 0)

        @pl.when(plain & special)
        def _():
            obuf[slot] = jnp.zeros((n, n), jnp.float32)

        if opening:

            @pl.when(first_tile & jnp.logical_not(special))
            def _():
                obuf[slot] = keep[a, col]

            @pl.when(first_tile & is_row0)
            def _():
                obuf[slot] = jnp.where(col == 0, l0_ref[...], 0.0)

            @pl.when(first_tile & is_row1)
            def _():
                obuf[slot] = jnp.where(col == 0, l10_ref[...], l1_ref[...])

        o_copy(k, slot).start()
        return carry

    lax.fori_loop(0, last, update, 0)
    o_copy(last - 2, lax.rem(last, 2)).wait()
    o_copy(last - 1, lax.rem(last + 1, 2)).wait()
    if opening:
        for copy in row_copies:
            copy.wait()


def finish(grid, blocks, factors, steps, sets, own=None, before=None):
    count, width, n, _ = blocks.shape
    opening = before is None
    total = len(steps) + (count if opening else 0)
    scalars = jnp.stack(
        [
            grid.core,
            (grid.lo == grid.core).astype(jnp.int32),
            grid.hi // grid.ys,
            (grid.row == 0).astype(jnp.int32),
            (grid.row == 1).astype(jnp.int32),
            grid.col,
        ]
    ).astype(jnp.int32)
    inputs = [scalars, blocks, *factors]
    if opening:
        inputs += own
    for group in sets:
        inputs += group
    aliases = {}
    if not opening:
        aliases[len(inputs)] = 0
        inputs += before
    anywhere = pl.BlockSpec(memory_space=pl.ANY)
    vmem = pl.BlockSpec(memory_space=pltpu.VMEM)
    result = jax.ShapeDtypeStruct(blocks.shape, jnp.float32)
    panel = jax.ShapeDtypeStruct((count, 2, n, n), jnp.bfloat16)
    half = pltpu.VMEM((n, n), jnp.bfloat16)
    pair = pltpu.VMEM((2, n, n), jnp.float32)
    panels = pltpu.VMEM((count + len(steps), 2, n, n), jnp.bfloat16)
    return pl.pallas_call(
        functools.partial(finish_kernel, (count, width, n), steps, opening),
        out_shape=[result, panel, panel] if opening else [result],
        in_specs=[pl.BlockSpec(memory_space=pltpu.SMEM), anywhere] + [vmem] * 5 + [anywhere] * (len(inputs) - 7),
        out_specs=[anywhere] * (3 if opening else 1),
        scratch_shapes=[
            pltpu.VMEM((total, 2, n, n), jnp.float32),
            panels,
            panels,
            pltpu.VMEM((count, 2, n, n), jnp.float32),
            half,
            half,
            half,
            half,
            half,
            half,
            pair,
            pair,
            pltpu.SemaphoreType.DMA((total, 2)),
            pltpu.SemaphoreType.DMA((2,)),
            pltpu.SemaphoreType.DMA((2,)),
            pltpu.SemaphoreType.DMA((2,)),
        ],
        input_output_aliases=aliases,
        cost_estimate=pl.CostEstimate(flops=20_000_000_000, bytes_accessed=60_000_000, transcendentals=0),
        compiler_params=pltpu.CompilerParams(vmem_limit_bytes=58 * 1024 * 1024),
    )(*inputs)


def shards(gram_tiles):
    blocks = gram_tiles[:, 0, :, 0]
    grid = Grid()
    n = blocks.shape[-1]
    slots = range(blocks.shape[0])
    raw = [blocks[a, 0] for a in slots]

    def up():
        return [
            grid.send(blocks[:, 0], lambda hi, lo, y, core: (hi, lo, h, core) if y == 0 else None)
            for h in range(1, grid.ys)
        ]

    def own_tile(a, got):
        tile = raw[a]
        for h in range(1, grid.ys):
            tile = jnp.where(grid.y == h, got[h - 1][a], tile)
        return tile

    def pair_start(tile):
        return [grid.swap_hi(tile, s) for s in range(1, grid.ys)]

    def pair_finish(tile, got):
        same = tile
        for s in range(1, grid.ys):
            same = jnp.where((grid.hi % grid.ys) ^ grid.y == s, got[s - 1], same)
        return same

    def cross(tile):
        if grid.ys == 2:
            return grid.send(tile, lambda hi, lo, y, core: (3 - hi, lo, y, core) if hi in (1, 2) else None)
        return grid.swap_hi(tile, grid.ys)

    def spread(tile):
        return grid.swap_hi(tile, 1) if grid.ys == 2 else tile

    def far_tile(middle, edge):
        return jnp.where((grid.hi == 1) | (grid.hi == 2), middle, edge) if grid.ys == 2 else middle

    part, sides = scatter(grid, raw[0])
    lifted = up()
    corner = merge(grid, *gather(grid, part))
    sides = gather(grid, after(sides, part))
    own = [own_tile(a, lifted) for a in slots]
    paired = [pair_start(own[0]), None]
    paired[1] = pair_start(own[1])
    x = after(unpack_lower(n, corner), *own)

    a, l, w = factor_open(x)

    got = lax.optimization_barrier((paired[0], a))[0]
    near = [pair_finish(own[0], got), None]
    middle = [cross(near[0]), None]
    near_x = [grid.swap_lo(near[0]), None]
    a = after(a, near[0])
    l0, w0 = factor_close(a, l, w)

    got, mid, sides = lax.optimization_barrier((paired[1], middle[0], sides, w0))[:3]
    middle[0] = mid
    near[1] = pair_finish(own[1], got)
    edge = [spread(middle[0]), None]
    middle[1] = cross(near[1])
    near_x[1] = grid.swap_lo(near[1])
    side0, side1 = unpack_sides(n, merge(grid, *sides))
    side0 = after(side0, near[1])
    l10, a, l, w = factor_corner(side0, side1, w0)

    eg, mid, nx = lax.optimization_barrier((edge[0], middle[1], near_x[0], a))[:3]
    edge[0], middle[1], near_x[0] = eg, mid, nx
    far = [far_tile(middle[0], edge[0]), None]
    edge[1] = spread(middle[1])
    far_x = [grid.swap_lo(far[0]), None]
    own_got = [grid.swap_core(after(own[k], a)) for k in slots]
    near_got = [grid.swap_core(after(near[k], a)) for k in slots]
    near_x_got = [grid.swap_core(near_x[0]), None]
    a = after(a, far[0])
    l1, w1 = factor_close(a, l, w)

    eg, fx, nx = lax.optimization_barrier((edge[1], far_x[0], near_x[1], w1))[:3]
    edge[1], far_x[0], near_x[1] = eg, fx, nx
    far[1] = far_tile(middle[1], edge[1])
    far_x[1] = grid.swap_lo(far[1])
    far_got = [grid.swap_core(far[k]) for k in slots]
    near_x_got[1] = grid.swap_core(near_x[1])
    far_x_got = [grid.swap_core(far_x[0]), None]
    factors = (l0, l10, l1, w0, after(w1, far[1]))

    def groups(k, far_one):
        if far_one:
            return [far[k], far_got[k], far_x[k], far_x_got[k]]
        return [near[k], near_got[k], near_x[k], near_x_got[k]]

    steps = [(k, f) for k in slots for f in (0, 1)]
    head, rest = tuple(steps[:-1]), tuple(steps[-1:])
    done = finish(grid, blocks, factors, head, [groups(*step) for step in head], [*own, *own_got])
    far_x[1] = after(far_x[1], done[0])
    far_x_got[1] = grid.swap_core(far_x[1])
    blocks = finish(grid, blocks, factors, rest, [groups(*step) for step in rest], before=list(done))[0]
    return blocks[:, None, :, None]


def solution(mesh):
    devices = mesh.devices
    mesh = jax.sharding.Mesh(devices.reshape(devices.shape[0], -1, 2), AXES)
    placed = P(None, "row", None, ("y", "core"), None, None)
    return jax.shard_map(shards, mesh=mesh, in_specs=(placed,), out_specs=placed, check_vma=False)
```

```python
import functools

import jax
import jax.numpy as jnp
from jax import lax
from jax.experimental import pallas as pl
from jax.experimental.pallas import tpu as pltpu
from jax.sharding import PartitionSpec as P

GROUP = 8
BLOCK = 128
AXES = ("row", "y", "core")


def contract(a, b, ca, cb, precision=lax.Precision.HIGHEST):
    return lax.dot_general(
        a, b, (((ca,), (cb,)), ((), ())), precision=precision, preferred_element_type=jnp.float32
    )


def factor_block(s_ref, e_ref, u_ref):
    n = s_ref.shape[0]
    sub = lax.broadcasted_iota(jnp.int32, (GROUP, n), 0)
    lane = lax.broadcasted_iota(jnp.int32, (GROUP, n), 1)
    down = lax.broadcasted_iota(jnp.int32, (n, n), 0)
    across = lax.broadcasted_iota(jnp.int32, (n, n), 1)
    e_ref[...] = (down == across).astype(jnp.float32)
    for start in range(0, n, GROUP):
        stop = start + GROUP
        tall = s_ref[start:stop, :]
        unit = e_ref[start:stop, :]
        entry = {}
        for j in range(GROUP):
            for i in range(j, GROUP):
                entry[i, j] = jnp.broadcast_to(tall[j : j + 1, start + i : start + i + 1], (1, n))
        rows = [tall[t : t + 1, :] for t in range(GROUP)]
        units = [unit[t : t + 1, :] for t in range(GROUP)]
        for t in range(GROUP):
            scale = lax.rsqrt(entry[t, t])
            for i in range(t + 1, GROUP):
                entry[i, t] = entry[i, t] * scale
            rows[t] = rows[t] * scale
            units[t] = units[t] * scale
            for i in range(t + 1, GROUP):
                for j in range(t + 1, i + 1):
                    entry[i, j] = entry[i, j] - entry[i, t] * entry[j, t]
                rows[i] = rows[i] - entry[i, t] * rows[t]
                units[i] = units[i] - entry[i, t] * units[t]
        u = jnp.where(lane >= sub + start, jnp.concatenate(rows, 0), 0.0)
        v = jnp.concatenate(units, 0)
        u_ref[start:stop, :] = u
        e_ref[start:stop, :] = v
        if stop < n:
            s_ref[stop:, :] = s_ref[stop:, :] - contract(u, u, 0, 0)[stop:, :]
            e_ref[stop:, :] = e_ref[stop:, :] - contract(u, v, 0, 0)[stop:, :]


def eliminate(first, last, a_ref, l_ref, w_ref, s_ref, e_ref, u_ref):
    def step(k):
        begin = k * BLOCK
        end = begin + BLOCK
        at = slice(begin, end)
        later = slice(end, a_ref.shape[0])
        inverse = e_ref[...]
        l_ref[at, at] = u_ref[...].T
        w_ref[at, at] = inverse
        if begin > 0:
            solved = contract(inverse, w_ref[at, :begin], 1, 0)
            w_ref[at, :begin] = solved
        if end < a_ref.shape[0]:
            below = contract(a_ref[later, at], inverse, 1, 1)
            l_ref[later, at] = below
            a_ref[later, later] -= contract(below, below, 1, 1)
            w_ref[later, at] = -contract(below, inverse, 1, 0)
            if begin > 0:
                w_ref[later, :begin] -= contract(below, solved, 1, 0)

    def body(k, carry):
        at = pl.ds(pl.multiple_of(k * BLOCK, BLOCK), BLOCK)
        s_ref[...] = a_ref[at, at]
        factor_block(s_ref, e_ref, u_ref)
        for known in range(first, last):

            @pl.when(k == known)
            def _():
                step(known)

        return carry

    lax.fori_loop(first, last, body, 0)


def open_kernel(last, x_ref, rest_ref, l_ref, w_ref, a_ref, *scratch):
    a_ref[...] = x_ref[...]
    l_ref[...] = jnp.zeros_like(l_ref)
    w_ref[...] = jnp.zeros_like(w_ref)
    eliminate(0, last, a_ref, l_ref, w_ref, *scratch)
    rest_ref[...] = a_ref[last * BLOCK :, last * BLOCK :]


def corner_kernel(last, side_ref, x_ref, inverse_ref, p_ref, rest_ref, l_ref, w_ref, a_ref, *scratch):
    n = x_ref.shape[0]
    half = n // 2

    def solve(c, carry):
        at = pl.ds(pl.multiple_of(c * half, half), half)
        p_ref[:, at] = contract(side_ref[...], inverse_ref[at, :], 1, 1)
        return carry

    def subtract(c, carry):
        at = pl.ds(pl.multiple_of(c * half, half), half)
        a_ref[:, at] = x_ref[:, at] - contract(p_ref[...], p_ref[at, :], 1, 1)
        return carry

    lax.fori_loop(0, 2, solve, 0)
    lax.fori_loop(0, 2, subtract, 0)
    l_ref[...] = jnp.zeros_like(l_ref)
    w_ref[...] = jnp.zeros_like(w_ref)
    eliminate(0, last, a_ref, l_ref, w_ref, *scratch)
    rest_ref[...] = a_ref[last * BLOCK :, last * BLOCK :]


def close_kernel(first, last, rest_ref, l_in, w_in, l_ref, w_ref, a_ref, *scratch):
    a_ref[first * BLOCK :, first * BLOCK :] = rest_ref[...]
    l_ref[...] = l_in[...]
    w_ref[...] = w_in[...]
    eliminate(first, last, a_ref, l_ref, w_ref, *scratch)


def call(kernel, n, inputs, outputs):
    small = pltpu.VMEM((BLOCK, BLOCK), jnp.float32)
    space = pl.BlockSpec(memory_space=pltpu.VMEM)
    return pl.pallas_call(
        kernel,
        out_shape=[jax.ShapeDtypeStruct((size, size), jnp.float32) for size in outputs],
        in_specs=[space] * len(inputs),
        out_specs=[space] * len(outputs),
        scratch_shapes=[pltpu.VMEM((n, n), jnp.float32), small, small, small],
        cost_estimate=pl.CostEstimate(flops=20_000_000_000, bytes_accessed=60_000_000, transcendentals=0),
    )(*inputs)


def halfway(n):
    return n // BLOCK // 2


def left(n):
    return n - halfway(n) * BLOCK


def factor_open(x):
    n = x.shape[0]
    return call(functools.partial(open_kernel, halfway(n)), n, (x,), (left(n), n, n))


def factor_corner(side, x, inverse):
    n = x.shape[0]
    return call(functools.partial(corner_kernel, halfway(n)), n, (side, x, inverse), (n, left(n), n, n))


def factor_close(rest, l, w):
    n = l.shape[0]
    return call(functools.partial(close_kernel, halfway(n), n // BLOCK), n, (rest, l, w), (n, n))


class Grid:
    def __init__(self):
        self.rows = lax.axis_size("row")
        self.ys = lax.axis_size("y")
        self.cols = self.ys * 2
        self.his = self.rows // 2
        self.row, self.y, self.core = [lax.axis_index(axis) for axis in AXES]
        self.col = self.y * 2 + self.core
        self.hi, self.lo = self.row // 2, self.row % 2

    def send(self, x, target):
        pairs = []
        for hi in range(self.his):
            for lo in range(2):
                for y in range(self.ys):
                    for core in range(2):
                        to = target(hi, lo, y, core)
                        if to is not None:
                            pairs.append((self.number(hi, lo, y, core), self.number(*to)))
        return lax.ppermute(x, AXES, pairs)

    def number(self, hi, lo, y, core):
        return (hi * 2 + lo) * self.cols + y * 2 + core

    def swap_lo(self, x):
        return self.send(x, lambda hi, lo, y, core: (hi, 1 - lo, y, core))

    def swap_core(self, x):
        return self.send(x, lambda hi, lo, y, core: (hi, lo, y, 1 - core))

    def swap_y(self, x, s):
        return self.send(x, lambda hi, lo, y, core: (hi, lo, y ^ s, core))

    def swap_hi(self, x, s):
        return self.send(x, lambda hi, lo, y, core: (hi ^ s, lo, y, core))


def after(x, *values):
    return lax.optimization_barrier((x, *values))[0]


def order_blocks(n):
    count = n // BLOCK
    lower = [(i, j) for i in range(count) for j in range(i + 1)]
    return lower, [(i, j) for i in range(count) for j in range(i + 1, count)]


def join(n, lookup):
    count = n // BLOCK
    zero = jnp.zeros((BLOCK, BLOCK), jnp.float32)
    return jnp.concatenate(
        [jnp.concatenate([lookup.get((i, j), zero) for j in range(count)], 1) for i in range(count)], 0
    )


def scatter(grid, tile):
    n = tile.shape[0]
    total = grid.rows * grid.cols
    parts = []
    for at in order_blocks(n):
        blocks = [tile[i * BLOCK : (i + 1) * BLOCK, j * BLOCK : (j + 1) * BLOCK] for i, j in at]
        parts.append(jnp.stack(blocks).reshape(total, -1, BLOCK))
    lower = parts[0].shape[1]
    got = lax.all_to_all(jnp.concatenate(parts, 1), AXES, 0, 0, tiled=True)
    corner, side, last = got[0, :lower], got[grid.cols], got[grid.cols + 1, :lower]
    return corner, jnp.concatenate([side, last], 0)


def gather(grid, part):
    spread = jnp.broadcast_to(part[None], (grid.rows * grid.ys, *part.shape))
    mine = lax.all_to_all(spread, ("row", "y"), 0, 0, tiled=True)
    return mine, grid.swap_core(mine)


def merge(grid, mine, other):
    even = grid.core == 0
    whole = jnp.stack([jnp.where(even, mine, other), jnp.where(even, other, mine)], 1)
    return whole.reshape(-1, *mine.shape[1:])


def unpack_lower(n, packed):
    lower, _ = order_blocks(n)
    packed = packed.reshape(len(lower), BLOCK, BLOCK)
    return join(n, {key: packed[k] for k, key in enumerate(lower)})


def unpack_sides(n, packed):
    lower, upper = order_blocks(n)
    rows = len(lower) * BLOCK // packed.shape[0]
    more = rows + len(upper) * BLOCK // packed.shape[0]
    low = packed[:, :rows].reshape(len(lower), BLOCK, BLOCK)
    high = packed[:, rows:more].reshape(len(upper), BLOCK, BLOCK)
    lookup = {key: low[k] for k, key in enumerate(lower)}
    lookup.update({key: high[k] for k, key in enumerate(upper)})
    return join(n, lookup), unpack_lower(n, packed[:, more:])


def split(x):
    high = x.astype(jnp.bfloat16)
    return high, (x - high.astype(jnp.float32)).astype(jnp.bfloat16)


def product(a, b, cb):
    def one(x, y):
        return lax.dot_general(x, y, (((1,), (cb,)), ((), ())), preferred_element_type=jnp.float32)

    return one(a[0], b[0]) + (one(a[0], b[1]) + one(a[1], b[0]))


def finish_kernel(shape, steps, opening, scalars, *refs):
    count, width, n = shape
    extra = count if opening else 0
    total = extra + len(steps)
    g_ref, l0_ref, l10_ref, l1_ref, w0_ref, w1_ref = refs[:6]
    refs = refs[6:]
    own = refs[: 2 * extra]
    refs = refs[2 * extra :]
    sets = [refs[4 * e : 4 * e + 4] for e in range(len(steps))]
    refs = refs[4 * len(steps) :]
    if not opening:
        _, rows_in = refs[0], refs[1:3]
        refs = refs[3:]
    out_ref = refs[0]
    rows_out = refs[1:3] if opening else ()
    refs = refs[3:] if opening else refs[1:]
    raw, high, low, keep, w0h, w0l, w1h, w1l, lh, ll, gbuf, obuf, rsem, gsem, osem, psem = refs
    core, same_lo, half, row0, row1, col = [scalars[k] for k in range(6)]

    def fetch(condition, ref, slot, panel):
        @pl.when(condition)
        def _():
            pltpu.make_async_copy(ref, raw.at[slot, panel], rsem.at[slot, panel]).start()

    for panel in range(2):
        for a in range(extra):
            fetch(core == panel, own[a], a, panel)
            fetch(core != panel, own[extra + a], a, panel)
    for e in range(len(steps)):
        straight, straight_got, crossed, crossed_got = sets[e]
        for panel in range(2):
            fetch((same_lo == 1) & (core == panel), straight, extra + e, panel)
            fetch((same_lo == 1) & (core != panel), straight_got, extra + e, panel)
            fetch((same_lo == 0) & (core == panel), crossed, extra + e, panel)
            fetch((same_lo == 0) & (core != panel), crossed_got, extra + e, panel)

    def column(e):
        slot = far = 0
        for at, (s, f) in enumerate(steps):
            slot = jnp.where(e == at, s, slot)
            far = jnp.where(e == at, f, far)
        return 2 * slot + jnp.where(far == 1, 1 - half, half)

    def place(k):
        return lax.rem(k, count), column(k // count)

    def g_copy(k, slot):
        a, t = place(k)
        return pltpu.make_async_copy(g_ref.at[a, t], gbuf.at[slot], gsem.at[slot])

    def o_copy(k, slot):
        a, t = place(k)
        return pltpu.make_async_copy(obuf.at[slot], out_ref.at[a, t], osem.at[slot])

    g_copy(0, 0).start()
    held = (high.at[:count], low.at[:count])
    if not opening:
        row_copies = [pltpu.make_async_copy(rows_in[k], held[k], psem.at[k]) for k in range(2)]
        for copy in row_copies:
            copy.start()
    w0h[...], w0l[...] = split(w0_ref[...])
    w1h[...], w1l[...] = split(w1_ref[...])
    lh[...], ll[...] = split(l10_ref[...])

    mid = n // 2

    def times_lower(x, yh, yl):
        head = product((x[0][:, :mid], x[1][:, :mid]), (yh[:mid, :mid], yl[:mid, :mid]), 1)
        return jnp.concatenate([head, product(x, (yh[mid:, :], yl[mid:, :]), 1)], 1)

    def solve(k, carry):
        at = k if opening else k + count
        pltpu.make_async_copy(sets[0][0], raw.at[k, 0], rsem.at[k, 0]).wait()
        p0 = times_lower(split(raw[k, 0]), w0h, w0l)
        high[at, 0], low[at, 0] = split(p0)
        pltpu.make_async_copy(sets[0][0], raw.at[k, 1], rsem.at[k, 1]).wait()

        def strip(c, carry):
            part = pl.ds(pl.multiple_of(c * mid, mid), mid)
            whole = (high[at, 0], low[at, 0])
            raw[k, 1, :, part] = raw[k, 1, :, part] - product(whole, (lh[part, :], ll[part, :]), 1)
            return carry

        lax.fori_loop(0, 2, strip, 0)
        p1 = times_lower(split(raw[k, 1]), w1h, w1l)
        high[at, 1], low[at, 1] = split(p1)
        if opening:

            @pl.when(k < count)
            def _():
                keep[k, 0] = p0
                keep[k, 1] = p1

        return carry

    lax.fori_loop(0, total, solve, 0)
    if opening:
        row_copies = [pltpu.make_async_copy(held[k], rows_out[k], psem.at[k]) for k in range(2)]
        for copy in row_copies:
            copy.start()
    else:
        for copy in row_copies:
            copy.wait()

    last = count * len(steps)

    def update(k, carry):
        slot = lax.rem(k, 2)
        a, t = place(k)
        e = k // count
        g_copy(k, slot).wait()

        @pl.when(k + 1 < last)
        def _():
            g_copy(k + 1, 1 - slot).start()

        @pl.when(k >= 2)
        def _():
            o_copy(k - 2, slot).wait()

        first_tile = (t == 0) & (col < 2) if opening else jnp.bool_(False)
        is_row0 = (a == 0) & (row0 == 1)
        is_row1 = (a == 0) & (row1 == 1)
        special = is_row0 | is_row1
        plain = jnp.logical_not(first_tile)

        @pl.when(plain & jnp.logical_not(special))
        def _():
            def strip(c, carry):
                at = pl.ds(pl.multiple_of(c * mid, mid), mid)
                value = gbuf[slot, :, at]
                for panel in range(2):
                    column_part = (high[count + e, panel, at, :], low[count + e, panel, at, :])
                    value = value - product((high[a, panel], low[a, panel]), column_part, 1)
                obuf[slot, :, at] = value
                return carry

            lax.fori_loop(0, 2, strip, 0)

        @pl.when(plain & special)
        def _():
            obuf[slot] = jnp.zeros((n, n), jnp.float32)

        if opening:

            @pl.when(first_tile & jnp.logical_not(special))
            def _():
                obuf[slot] = keep[a, col]

            @pl.when(first_tile & is_row0)
            def _():
                obuf[slot] = jnp.where(col == 0, l0_ref[...], 0.0)

            @pl.when(first_tile & is_row1)
            def _():
                obuf[slot] = jnp.where(col == 0, l10_ref[...], l1_ref[...])

        o_copy(k, slot).start()
        return carry

    lax.fori_loop(0, last, update, 0)
    o_copy(last - 2, lax.rem(last, 2)).wait()
    o_copy(last - 1, lax.rem(last + 1, 2)).wait()
    if opening:
        for copy in row_copies:
            copy.wait()


def finish(grid, blocks, factors, steps, sets, own=None, before=None):
    count, width, n, _ = blocks.shape
    opening = before is None
    total = len(steps) + (count if opening else 0)
    scalars = jnp.stack(
        [
            grid.core,
            (grid.lo == grid.core).astype(jnp.int32),
            grid.hi // grid.ys,
            (grid.row == 0).astype(jnp.int32),
            (grid.row == 1).astype(jnp.int32),
            grid.col,
        ]
    ).astype(jnp.int32)
    inputs = [scalars, blocks, *factors]
    if opening:
        inputs += own
    for group in sets:
        inputs += group
    aliases = {}
    if not opening:
        aliases[len(inputs)] = 0
        inputs += before
    anywhere = pl.BlockSpec(memory_space=pl.ANY)
    vmem = pl.BlockSpec(memory_space=pltpu.VMEM)
    result = jax.ShapeDtypeStruct(blocks.shape, jnp.float32)
    panel = jax.ShapeDtypeStruct((count, 2, n, n), jnp.bfloat16)
    half = pltpu.VMEM((n, n), jnp.bfloat16)
    pair = pltpu.VMEM((2, n, n), jnp.float32)
    panels = pltpu.VMEM((count + len(steps), 2, n, n), jnp.bfloat16)
    return pl.pallas_call(
        functools.partial(finish_kernel, (count, width, n), steps, opening),
        out_shape=[result, panel, panel] if opening else [result],
        in_specs=[pl.BlockSpec(memory_space=pltpu.SMEM), anywhere] + [vmem] * 5 + [anywhere] * (len(inputs) - 7),
        out_specs=[anywhere] * (3 if opening else 1),
        scratch_shapes=[
            pltpu.VMEM((total, 2, n, n), jnp.float32),
            panels,
            panels,
            pltpu.VMEM((count, 2, n, n), jnp.float32),
            half,
            half,
            half,
            half,
            half,
            half,
            pair,
            pair,
            pltpu.SemaphoreType.DMA((total, 2)),
            pltpu.SemaphoreType.DMA((2,)),
            pltpu.SemaphoreType.DMA((2,)),
            pltpu.SemaphoreType.DMA((2,)),
        ],
        input_output_aliases=aliases,
        cost_estimate=pl.CostEstimate(flops=20_000_000_000, bytes_accessed=60_000_000, transcendentals=0),
        compiler_params=pltpu.CompilerParams(vmem_limit_bytes=58 * 1024 * 1024),
    )(*inputs)


def shards(gram_tiles):
    blocks = gram_tiles[:, 0, :, 0]
    grid = Grid()
    n = blocks.shape[-1]
    slots = range(blocks.shape[0])
    raw = [blocks[a, 0] for a in slots]

    def up(a):
        return [grid.send(raw[a], lambda hi, lo, y, core: (hi, lo, h, core) if y == 0 else None) for h in range(1, grid.ys)]

    def own_tile(a, got):
        tile = raw[a]
        for h in range(1, grid.ys):
            tile = jnp.where(grid.y == h, got[h - 1], tile)
        return tile

    def pair_start(tile):
        return [grid.swap_hi(tile, s) for s in range(1, grid.ys)]

    def pair_finish(tile, got):
        same = tile
        for s in range(1, grid.ys):
            same = jnp.where((grid.hi % grid.ys) ^ grid.y == s, got[s - 1], same)
        return same

    def cross(tile):
        if grid.ys == 2:
            return grid.send(tile, lambda hi, lo, y, core: (3 - hi, lo, y, core) if hi in (1, 2) else None)
        return grid.swap_hi(tile, grid.ys)

    def spread(tile):
        return grid.swap_hi(tile, 1) if grid.ys == 2 else tile

    def far_tile(middle, edge):
        return jnp.where((grid.hi == 1) | (grid.hi == 2), middle, edge) if grid.ys == 2 else middle

    part, sides = scatter(grid, raw[0])
    lifted = [up(a) for a in slots]
    corner = merge(grid, *gather(grid, part))
    sides = gather(grid, after(sides, part))
    own = [own_tile(0, lifted[0]), None]
    paired = [pair_start(own[0]), None]
    x = after(unpack_lower(n, corner), own[0])

    a, l, w = factor_open(x)

    got, lift = lax.optimization_barrier((paired[0], lifted[1], a))[:2]
    near = [pair_finish(own[0], got), None]
    own[1] = own_tile(1, lift)
    middle = [cross(near[0]), None]
    paired[1] = pair_start(own[1])
    near_x = [grid.swap_lo(near[0]), None]
    a = after(a, near[0], own[1])
    l0, w0 = factor_close(a, l, w)

    got, mid, sides = lax.optimization_barrier((paired[1], middle[0], sides, w0))[:3]
    middle[0] = mid
    near[1] = pair_finish(own[1], got)
    edge = [spread(middle[0]), None]
    middle[1] = cross(near[1])
    near_x[1] = grid.swap_lo(near[1])
    side0, side1 = unpack_sides(n, merge(grid, *sides))
    side0 = after(side0, near[1])
    l10, a, l, w = factor_corner(side0, side1, w0)

    eg, mid, nx = lax.optimization_barrier((edge[0], middle[1], near_x[0], a))[:3]
    edge[0], middle[1], near_x[0] = eg, mid, nx
    far = [far_tile(middle[0], edge[0]), None]
    edge[1] = spread(middle[1])
    far_x = [grid.swap_lo(far[0]), None]
    own_got = [grid.swap_core(after(own[k], a)) for k in slots]
    near_got = [grid.swap_core(after(near[k], a)) for k in slots]
    near_x_got = [grid.swap_core(near_x[0]), None]
    a = after(a, far[0])
    l1, w1 = factor_close(a, l, w)

    eg, fx, nx = lax.optimization_barrier((edge[1], far_x[0], near_x[1], w1))[:3]
    edge[1], far_x[0], near_x[1] = eg, fx, nx
    far[1] = far_tile(middle[1], edge[1])
    far_x[1] = grid.swap_lo(far[1])
    far_got = [grid.swap_core(far[k]) for k in slots]
    near_x_got[1] = grid.swap_core(near_x[1])
    far_x_got = [grid.swap_core(far_x[0]), None]
    factors = (l0, l10, l1, w0, after(w1, far[1]))

    def groups(k, far_one):
        if far_one:
            return [far[k], far_got[k], far_x[k], far_x_got[k]]
        return [near[k], near_got[k], near_x[k], near_x_got[k]]

    steps = [(k, f) for k in slots for f in (0, 1)]
    head, rest = tuple(steps[:-1]), tuple(steps[-1:])
    done = finish(grid, blocks, factors, head, [groups(*step) for step in head], [*own, *own_got])
    far_x[1] = after(far_x[1], done[0])
    far_x_got[1] = grid.swap_core(far_x[1])
    blocks = finish(grid, blocks, factors, rest, [groups(*step) for step in rest], before=list(done))[0]
    return blocks[:, None, :, None]


def solution(mesh):
    devices = mesh.devices
    mesh = jax.sharding.Mesh(devices.reshape(devices.shape[0], -1, 2), AXES)
    placed = P(None, "row", None, ("y", "core"), None, None)
    return jax.shard_map(shards, mesh=mesh, in_specs=(placed,), out_specs=placed, check_vma=False)
```

```python
import functools

import jax
import jax.numpy as jnp
from jax import lax
from jax.experimental import pallas as pl
from jax.experimental.pallas import tpu as pltpu
from jax.sharding import PartitionSpec as P

GROUP = 8
BLOCK = 128
AXES = ("row", "y", "core")


def contract(a, b, ca, cb, precision=lax.Precision.HIGHEST):
    return lax.dot_general(
        a, b, (((ca,), (cb,)), ((), ())), precision=precision, preferred_element_type=jnp.float32
    )


def factor_block(s_ref, e_ref, u_ref):
    n = s_ref.shape[0]
    sub = lax.broadcasted_iota(jnp.int32, (GROUP, n), 0)
    lane = lax.broadcasted_iota(jnp.int32, (GROUP, n), 1)
    down = lax.broadcasted_iota(jnp.int32, (n, n), 0)
    across = lax.broadcasted_iota(jnp.int32, (n, n), 1)
    e_ref[...] = (down == across).astype(jnp.float32)
    for start in range(0, n, GROUP):
        stop = start + GROUP
        tall = s_ref[start:stop, :]
        unit = e_ref[start:stop, :]
        entry = {}
        for j in range(GROUP):
            for i in range(j, GROUP):
                entry[i, j] = jnp.broadcast_to(tall[j : j + 1, start + i : start + i + 1], (1, n))
        rows = [tall[t : t + 1, :] for t in range(GROUP)]
        units = [unit[t : t + 1, :] for t in range(GROUP)]
        for t in range(GROUP):
            scale = lax.rsqrt(entry[t, t])
            for i in range(t + 1, GROUP):
                entry[i, t] = entry[i, t] * scale
            rows[t] = rows[t] * scale
            units[t] = units[t] * scale
            for i in range(t + 1, GROUP):
                for j in range(t + 1, i + 1):
                    entry[i, j] = entry[i, j] - entry[i, t] * entry[j, t]
                rows[i] = rows[i] - entry[i, t] * rows[t]
                units[i] = units[i] - entry[i, t] * units[t]
        u = jnp.where(lane >= sub + start, jnp.concatenate(rows, 0), 0.0)
        v = jnp.concatenate(units, 0)
        u_ref[start:stop, :] = u
        e_ref[start:stop, :] = v
        if stop < n:
            s_ref[stop:, :] = s_ref[stop:, :] - contract(u, u, 0, 0)[stop:, :]
            e_ref[stop:, :] = e_ref[stop:, :] - contract(u, v, 0, 0)[stop:, :]


def eliminate(first, last, a_ref, l_ref, w_ref, s_ref, e_ref, u_ref):
    def step(k):
        begin = k * BLOCK
        end = begin + BLOCK
        at = slice(begin, end)
        later = slice(end, a_ref.shape[0])
        inverse = e_ref[...]
        l_ref[at, at] = u_ref[...].T
        w_ref[at, at] = inverse
        if begin > 0:
            solved = contract(inverse, w_ref[at, :begin], 1, 0)
            w_ref[at, :begin] = solved
        if end < a_ref.shape[0]:
            below = contract(a_ref[later, at], inverse, 1, 1)
            l_ref[later, at] = below
            a_ref[later, later] -= contract(below, below, 1, 1)
            w_ref[later, at] = -contract(below, inverse, 1, 0)
            if begin > 0:
                w_ref[later, :begin] -= contract(below, solved, 1, 0)

    def body(k, carry):
        at = pl.ds(pl.multiple_of(k * BLOCK, BLOCK), BLOCK)
        s_ref[...] = a_ref[at, at]
        factor_block(s_ref, e_ref, u_ref)
        for known in range(first, last):

            @pl.when(k == known)
            def _():
                step(known)

        return carry

    lax.fori_loop(first, last, body, 0)


def open_kernel(last, x_ref, rest_ref, l_ref, w_ref, a_ref, *scratch):
    a_ref[...] = x_ref[...]
    l_ref[...] = jnp.zeros_like(l_ref)
    w_ref[...] = jnp.zeros_like(w_ref)
    eliminate(0, last, a_ref, l_ref, w_ref, *scratch)
    rest_ref[...] = a_ref[last * BLOCK :, last * BLOCK :]


def corner_kernel(last, side_ref, x_ref, inverse_ref, p_ref, rest_ref, l_ref, w_ref, a_ref, *scratch):
    n = x_ref.shape[0]
    half = n // 2

    def solve(c, carry):
        at = pl.ds(pl.multiple_of(c * half, half), half)
        p_ref[:, at] = contract(side_ref[...], inverse_ref[at, :], 1, 1)
        return carry

    def subtract(c, carry):
        at = pl.ds(pl.multiple_of(c * half, half), half)
        a_ref[:, at] = x_ref[:, at] - contract(p_ref[...], p_ref[at, :], 1, 1)
        return carry

    lax.fori_loop(0, 2, solve, 0)
    lax.fori_loop(0, 2, subtract, 0)
    l_ref[...] = jnp.zeros_like(l_ref)
    w_ref[...] = jnp.zeros_like(w_ref)
    eliminate(0, last, a_ref, l_ref, w_ref, *scratch)
    rest_ref[...] = a_ref[last * BLOCK :, last * BLOCK :]


def close_kernel(first, last, rest_ref, l_in, w_in, l_ref, w_ref, a_ref, *scratch):
    a_ref[first * BLOCK :, first * BLOCK :] = rest_ref[...]
    l_ref[...] = l_in[...]
    w_ref[...] = w_in[...]
    eliminate(first, last, a_ref, l_ref, w_ref, *scratch)


def call(kernel, n, inputs, outputs):
    small = pltpu.VMEM((BLOCK, BLOCK), jnp.float32)
    space = pl.BlockSpec(memory_space=pltpu.VMEM)
    return pl.pallas_call(
        kernel,
        out_shape=[jax.ShapeDtypeStruct((size, size), jnp.float32) for size in outputs],
        in_specs=[space] * len(inputs),
        out_specs=[space] * len(outputs),
        scratch_shapes=[pltpu.VMEM((n, n), jnp.float32), small, small, small],
        cost_estimate=pl.CostEstimate(flops=20_000_000_000, bytes_accessed=60_000_000, transcendentals=0),
    )(*inputs)


def halfway(n):
    return n // BLOCK // 2


def left(n):
    return n - halfway(n) * BLOCK


def factor_open(x):
    n = x.shape[0]
    return call(functools.partial(open_kernel, halfway(n)), n, (x,), (left(n), n, n))


def factor_corner(side, x, inverse):
    n = x.shape[0]
    return call(functools.partial(corner_kernel, halfway(n)), n, (side, x, inverse), (n, left(n), n, n))


def factor_close(rest, l, w):
    n = l.shape[0]
    return call(functools.partial(close_kernel, halfway(n), n // BLOCK), n, (rest, l, w), (n, n))


class Grid:
    def __init__(self):
        self.rows = lax.axis_size("row")
        self.ys = lax.axis_size("y")
        self.cols = self.ys * 2
        self.his = self.rows // 2
        self.row, self.y, self.core = [lax.axis_index(axis) for axis in AXES]
        self.col = self.y * 2 + self.core
        self.hi, self.lo = self.row // 2, self.row % 2

    def send(self, x, target):
        pairs = []
        for hi in range(self.his):
            for lo in range(2):
                for y in range(self.ys):
                    for core in range(2):
                        to = target(hi, lo, y, core)
                        if to is not None:
                            pairs.append((self.number(hi, lo, y, core), self.number(*to)))
        return lax.ppermute(x, AXES, pairs)

    def number(self, hi, lo, y, core):
        return (hi * 2 + lo) * self.cols + y * 2 + core

    def swap_lo(self, x):
        return self.send(x, lambda hi, lo, y, core: (hi, 1 - lo, y, core))

    def swap_core(self, x):
        return self.send(x, lambda hi, lo, y, core: (hi, lo, y, 1 - core))

    def swap_y(self, x, s):
        return self.send(x, lambda hi, lo, y, core: (hi, lo, y ^ s, core))

    def swap_hi(self, x, s):
        return self.send(x, lambda hi, lo, y, core: (hi ^ s, lo, y, core))


def after(x, *values):
    return lax.optimization_barrier((x, *values))[0]


def order_blocks(n):
    count = n // BLOCK
    lower = [(i, j) for i in range(count) for j in range(i + 1)]
    return lower, [(i, j) for i in range(count) for j in range(i + 1, count)]


def join(n, lookup):
    count = n // BLOCK
    zero = jnp.zeros((BLOCK, BLOCK), jnp.float32)
    return jnp.concatenate(
        [jnp.concatenate([lookup.get((i, j), zero) for j in range(count)], 1) for i in range(count)], 0
    )


def scatter(grid, tile):
    n = tile.shape[0]
    total = grid.rows * grid.cols
    parts = []
    for at in order_blocks(n):
        blocks = [tile[i * BLOCK : (i + 1) * BLOCK, j * BLOCK : (j + 1) * BLOCK] for i, j in at]
        parts.append(jnp.stack(blocks).reshape(total, -1, BLOCK))
    lower = parts[0].shape[1]
    got = lax.all_to_all(jnp.concatenate(parts, 1), AXES, 0, 0, tiled=True)
    corner, side, last = got[0, :lower], got[grid.cols], got[grid.cols + 1, :lower]
    return corner, jnp.concatenate([side, last], 0)


def gather(grid, part):
    spread = jnp.broadcast_to(part[None], (grid.rows * grid.ys, *part.shape))
    mine = lax.all_to_all(spread, ("row", "y"), 0, 0, tiled=True)
    return mine, grid.swap_core(mine)


def merge(grid, mine, other):
    even = grid.core == 0
    whole = jnp.stack([jnp.where(even, mine, other), jnp.where(even, other, mine)], 1)
    return whole.reshape(-1, *mine.shape[1:])


def unpack_lower(n, packed):
    lower, _ = order_blocks(n)
    packed = packed.reshape(len(lower), BLOCK, BLOCK)
    return join(n, {key: packed[k] for k, key in enumerate(lower)})


def unpack_sides(n, packed):
    lower, upper = order_blocks(n)
    rows = len(lower) * BLOCK // packed.shape[0]
    more = rows + len(upper) * BLOCK // packed.shape[0]
    low = packed[:, :rows].reshape(len(lower), BLOCK, BLOCK)
    high = packed[:, rows:more].reshape(len(upper), BLOCK, BLOCK)
    lookup = {key: low[k] for k, key in enumerate(lower)}
    lookup.update({key: high[k] for k, key in enumerate(upper)})
    return join(n, lookup), unpack_lower(n, packed[:, more:])


def split(x):
    high = x.astype(jnp.bfloat16)
    return high, (x - high.astype(jnp.float32)).astype(jnp.bfloat16)


def product(*pairs):
    left, right = [], []
    for a, b in pairs:
        left += [a[0], a[0], a[1]]
        right += [b[0], b[1], b[0]]
    return lax.dot_general(
        jnp.concatenate(left, 1),
        jnp.concatenate(right, 1),
        (((1,), (1,)), ((), ())),
        preferred_element_type=jnp.float32,
    )


def finish_kernel(shape, steps, opening, scalars, *refs):
    count, width, n = shape
    extra = count if opening else 0
    total = extra + len(steps)
    g_ref, l0_ref, l10_ref, l1_ref, w0_ref, w1_ref = refs[:6]
    refs = refs[6:]
    own = refs[: 2 * extra]
    refs = refs[2 * extra :]
    sets = [refs[4 * e : 4 * e + 4] for e in range(len(steps))]
    refs = refs[4 * len(steps) :]
    if not opening:
        _, rows_in = refs[0], refs[1:3]
        refs = refs[3:]
    out_ref = refs[0]
    rows_out = refs[1:3] if opening else ()
    refs = refs[3:] if opening else refs[1:]
    raw, high, low, keep, w0h, w0l, w1h, w1l, lh, ll, gbuf, obuf, rsem, gsem, osem, psem = refs
    core, same_lo, half, row0, row1, col = [scalars[k] for k in range(6)]

    def fetch(condition, ref, slot, panel):
        @pl.when(condition)
        def _():
            pltpu.make_async_copy(ref, raw.at[slot, panel], rsem.at[slot, panel]).start()

    for panel in range(2):
        for a in range(extra):
            fetch(core == panel, own[a], a, panel)
            fetch(core != panel, own[extra + a], a, panel)
    for e in range(len(steps)):
        straight, straight_got, crossed, crossed_got = sets[e]
        for panel in range(2):
            fetch((same_lo == 1) & (core == panel), straight, extra + e, panel)
            fetch((same_lo == 1) & (core != panel), straight_got, extra + e, panel)
            fetch((same_lo == 0) & (core == panel), crossed, extra + e, panel)
            fetch((same_lo == 0) & (core != panel), crossed_got, extra + e, panel)

    def column(e):
        slot = far = 0
        for at, (s, f) in enumerate(steps):
            slot = jnp.where(e == at, s, slot)
            far = jnp.where(e == at, f, far)
        return 2 * slot + jnp.where(far == 1, 1 - half, half)

    def place(k):
        return lax.rem(k, count), column(k // count)

    def g_copy(k, slot):
        a, t = place(k)
        return pltpu.make_async_copy(g_ref.at[a, t], gbuf.at[slot], gsem.at[slot])

    def o_copy(k, slot):
        a, t = place(k)
        return pltpu.make_async_copy(obuf.at[slot], out_ref.at[a, t], osem.at[slot])

    g_copy(0, 0).start()
    held = (high.at[:count], low.at[:count])
    if not opening:
        row_copies = [pltpu.make_async_copy(rows_in[k], held[k], psem.at[k]) for k in range(2)]
        for copy in row_copies:
            copy.start()
    w0h[...], w0l[...] = split(w0_ref[...])
    w1h[...], w1l[...] = split(w1_ref[...])
    lh[...], ll[...] = split(l10_ref[...])

    mid = n // 2

    def times_lower(x, yh, yl):
        head = product(((x[0][:, :mid], x[1][:, :mid]), (yh[:mid, :mid], yl[:mid, :mid])))
        return jnp.concatenate([head, product((x, (yh[mid:, :], yl[mid:, :])))], 1)

    def solve(k, carry):
        at = k if opening else k + count
        pltpu.make_async_copy(sets[0][0], raw.at[k, 0], rsem.at[k, 0]).wait()
        p0 = times_lower(split(raw[k, 0]), w0h, w0l)
        high[at, 0], low[at, 0] = split(p0)
        pltpu.make_async_copy(sets[0][0], raw.at[k, 1], rsem.at[k, 1]).wait()

        def strip(c, carry):
            part = pl.ds(pl.multiple_of(c * mid, mid), mid)
            whole = (high[at, 0], low[at, 0])
            raw[k, 1, :, part] = raw[k, 1, :, part] - product((whole, (lh[part, :], ll[part, :])))
            return carry

        lax.fori_loop(0, 2, strip, 0)
        p1 = times_lower(split(raw[k, 1]), w1h, w1l)
        high[at, 1], low[at, 1] = split(p1)
        if opening:

            @pl.when(k < count)
            def _():
                keep[k, 0] = p0
                keep[k, 1] = p1

        return carry

    lax.fori_loop(0, total, solve, 0)
    if opening:
        row_copies = [pltpu.make_async_copy(held[k], rows_out[k], psem.at[k]) for k in range(2)]
        for copy in row_copies:
            copy.start()
    else:
        for copy in row_copies:
            copy.wait()

    last = count * len(steps)

    def update(k, carry):
        slot = lax.rem(k, 2)
        a, t = place(k)
        e = k // count
        g_copy(k, slot).wait()

        @pl.when(k + 1 < last)
        def _():
            g_copy(k + 1, 1 - slot).start()

        @pl.when(k >= 2)
        def _():
            o_copy(k - 2, slot).wait()

        first_tile = (t == 0) & (col < 2) if opening else jnp.bool_(False)
        is_row0 = (a == 0) & (row0 == 1)
        is_row1 = (a == 0) & (row1 == 1)
        special = is_row0 | is_row1
        plain = jnp.logical_not(first_tile)

        @pl.when(plain & jnp.logical_not(special))
        def _():
            def strip(c, carry):
                at = pl.ds(pl.multiple_of(c * mid, mid), mid)
                pairs = []
                for panel in range(2):
                    column_part = (high[count + e, panel, at, :], low[count + e, panel, at, :])
                    pairs.append(((high[a, panel], low[a, panel]), column_part))
                obuf[slot, :, at] = gbuf[slot, :, at] - product(*pairs)
                return carry

            lax.fori_loop(0, 2, strip, 0)

        @pl.when(plain & special)
        def _():
            obuf[slot] = jnp.zeros((n, n), jnp.float32)

        if opening:

            @pl.when(first_tile & jnp.logical_not(special))
            def _():
                obuf[slot] = keep[a, col]

            @pl.when(first_tile & is_row0)
            def _():
                obuf[slot] = jnp.where(col == 0, l0_ref[...], 0.0)

            @pl.when(first_tile & is_row1)
            def _():
                obuf[slot] = jnp.where(col == 0, l10_ref[...], l1_ref[...])

        o_copy(k, slot).start()
        return carry

    lax.fori_loop(0, last, update, 0)
    o_copy(last - 2, lax.rem(last, 2)).wait()
    o_copy(last - 1, lax.rem(last + 1, 2)).wait()
    if opening:
        for copy in row_copies:
            copy.wait()


def finish(grid, blocks, factors, steps, sets, own=None, before=None):
    count, width, n, _ = blocks.shape
    opening = before is None
    total = len(steps) + (count if opening else 0)
    scalars = jnp.stack(
        [
            grid.core,
            (grid.lo == grid.core).astype(jnp.int32),
            grid.hi // grid.ys,
            (grid.row == 0).astype(jnp.int32),
            (grid.row == 1).astype(jnp.int32),
            grid.col,
        ]
    ).astype(jnp.int32)
    inputs = [scalars, blocks, *factors]
    if opening:
        inputs += own
    for group in sets:
        inputs += group
    aliases = {}
    if not opening:
        aliases[len(inputs)] = 0
        inputs += before
    anywhere = pl.BlockSpec(memory_space=pl.ANY)
    vmem = pl.BlockSpec(memory_space=pltpu.VMEM)
    result = jax.ShapeDtypeStruct(blocks.shape, jnp.float32)
    panel = jax.ShapeDtypeStruct((count, 2, n, n), jnp.bfloat16)
    half = pltpu.VMEM((n, n), jnp.bfloat16)
    pair = pltpu.VMEM((2, n, n), jnp.float32)
    panels = pltpu.VMEM((count + len(steps), 2, n, n), jnp.bfloat16)
    return pl.pallas_call(
        functools.partial(finish_kernel, (count, width, n), steps, opening),
        out_shape=[result, panel, panel] if opening else [result],
        in_specs=[pl.BlockSpec(memory_space=pltpu.SMEM), anywhere] + [vmem] * 5 + [anywhere] * (len(inputs) - 7),
        out_specs=[anywhere] * (3 if opening else 1),
        scratch_shapes=[
            pltpu.VMEM((total, 2, n, n), jnp.float32),
            panels,
            panels,
            pltpu.VMEM((count, 2, n, n), jnp.float32),
            half,
            half,
            half,
            half,
            half,
            half,
            pair,
            pair,
            pltpu.SemaphoreType.DMA((total, 2)),
            pltpu.SemaphoreType.DMA((2,)),
            pltpu.SemaphoreType.DMA((2,)),
            pltpu.SemaphoreType.DMA((2,)),
        ],
        input_output_aliases=aliases,
        cost_estimate=pl.CostEstimate(flops=20_000_000_000, bytes_accessed=60_000_000, transcendentals=0),
        compiler_params=pltpu.CompilerParams(vmem_limit_bytes=58 * 1024 * 1024),
    )(*inputs)


def shards(gram_tiles):
    blocks = gram_tiles[:, 0, :, 0]
    grid = Grid()
    n = blocks.shape[-1]
    slots = range(blocks.shape[0])
    raw = [blocks[a, 0] for a in slots]

    def up(a):
        return [grid.send(raw[a], lambda hi, lo, y, core: (hi, lo, h, core) if y == 0 else None) for h in range(1, grid.ys)]

    def own_tile(a, got):
        tile = raw[a]
        for h in range(1, grid.ys):
            tile = jnp.where(grid.y == h, got[h - 1], tile)
        return tile

    def pair_start(tile):
        return [grid.swap_hi(tile, s) for s in range(1, grid.ys)]

    def pair_finish(tile, got):
        same = tile
        for s in range(1, grid.ys):
            same = jnp.where((grid.hi % grid.ys) ^ grid.y == s, got[s - 1], same)
        return same

    def cross(tile):
        if grid.ys == 2:
            return grid.send(tile, lambda hi, lo, y, core: (3 - hi, lo, y, core) if hi in (1, 2) else None)
        return grid.swap_hi(tile, grid.ys)

    def spread(tile):
        return grid.swap_hi(tile, 1) if grid.ys == 2 else tile

    def far_tile(middle, edge):
        return jnp.where((grid.hi == 1) | (grid.hi == 2), middle, edge) if grid.ys == 2 else middle

    part, sides = scatter(grid, raw[0])
    lifted = [up(a) for a in slots]
    corner = merge(grid, *gather(grid, part))
    sides = gather(grid, after(sides, part))
    own = [own_tile(0, lifted[0]), None]
    paired = [pair_start(own[0]), None]
    x = after(unpack_lower(n, corner), own[0])

    a, l, w = factor_open(x)

    got, lift = lax.optimization_barrier((paired[0], lifted[1], a))[:2]
    near = [pair_finish(own[0], got), None]
    own[1] = own_tile(1, lift)
    middle = [cross(near[0]), None]
    paired[1] = pair_start(own[1])
    near_x = [grid.swap_lo(near[0]), None]
    a = after(a, near[0], own[1])
    l0, w0 = factor_close(a, l, w)

    got, mid, sides = lax.optimization_barrier((paired[1], middle[0], sides, w0))[:3]
    middle[0] = mid
    near[1] = pair_finish(own[1], got)
    edge = [spread(middle[0]), None]
    middle[1] = cross(near[1])
    near_x[1] = grid.swap_lo(near[1])
    side0, side1 = unpack_sides(n, merge(grid, *sides))
    side0 = after(side0, near[1])
    l10, a, l, w = factor_corner(side0, side1, w0)

    eg, mid, nx = lax.optimization_barrier((edge[0], middle[1], near_x[0], a))[:3]
    edge[0], middle[1], near_x[0] = eg, mid, nx
    far = [far_tile(middle[0], edge[0]), None]
    edge[1] = spread(middle[1])
    far_x = [grid.swap_lo(far[0]), None]
    own_got = [grid.swap_core(after(own[k], a)) for k in slots]
    near_got = [grid.swap_core(after(near[k], a)) for k in slots]
    near_x_got = [grid.swap_core(near_x[0]), None]
    a = after(a, far[0])
    l1, w1 = factor_close(a, l, w)

    eg, fx, nx = lax.optimization_barrier((edge[1], far_x[0], near_x[1], w1))[:3]
    edge[1], far_x[0], near_x[1] = eg, fx, nx
    far[1] = far_tile(middle[1], edge[1])
    far_x[1] = grid.swap_lo(far[1])
    far_got = [grid.swap_core(far[k]) for k in slots]
    near_x_got[1] = grid.swap_core(near_x[1])
    far_x_got = [grid.swap_core(far_x[0]), None]
    factors = (l0, l10, l1, w0, after(w1, far[1]))

    def groups(k, far_one):
        if far_one:
            return [far[k], far_got[k], far_x[k], far_x_got[k]]
        return [near[k], near_got[k], near_x[k], near_x_got[k]]

    steps = [(k, f) for k in slots for f in (0, 1)]
    head, rest = tuple(steps[:-1]), tuple(steps[-1:])
    done = finish(grid, blocks, factors, head, [groups(*step) for step in head], [*own, *own_got])
    far_x[1] = after(far_x[1], done[0])
    far_x_got[1] = grid.swap_core(far_x[1])
    blocks = finish(grid, blocks, factors, rest, [groups(*step) for step in rest], before=list(done))[0]
    return blocks[:, None, :, None]


def solution(mesh):
    devices = mesh.devices
    mesh = jax.sharding.Mesh(devices.reshape(devices.shape[0], -1, 2), AXES)
    placed = P(None, "row", None, ("y", "core"), None, None)
    return jax.shard_map(shards, mesh=mesh, in_specs=(placed,), out_specs=placed, check_vma=False)
```
